32 devices in a mesh: cp: 4 (over y, x), grp: 8 (over z, core).
Axes of the slice: x: 2, y: 2, z: 4, core: 2. Of those that a mesh axis runs over, the one named last changes fastest.
Arguments:
- queries: bfloat16 [16, 512, 2048], P('grp', 'cp'), may hold values from -108 to 108
- keys: bfloat16 [16, 512, 2048], P('grp', 'cp'), may hold values from -4 to 4
- values: bfloat16 [16, 512, 2048], P('grp', 'cp'), may hold values from -6 to 6
- lengths: int32 [16], P('grp'), may hold values from 128 to 512
- frame_map: bfloat16 [2048, 2176], replicated, may hold values from -0.125 to 0.125
- proj_weight: bfloat16 [2176, 4096], P('grp', 'cp'), may hold values from -0.125 to 0.125
- head_weight: bfloat16 [4096, 256], P('cp'), may hold values from -0.375 to 0.375
- act_embed: float32 [7, 4096], P(None, 'cp'), may hold values from -0.5 to 0.5
- actions: int32 [16, 7], P('grp'), may hold values from 0 to 255
- action_mask: int32 [16, 7], P('grp'), may hold values 0 or 1
- group_ids: int32 [16], P('grp'), may hold values from 0 to 1
- rewards: float32 [16], P('grp'), may hold values from -6 to 6
Outputs:
- logprobs: float32 [16, 7], P('grp')
- grad_proj: bfloat16 [2176, 4096], P('grp', 'cp')
- grad_head: bfloat16 [4096, 256], P('cp')
The draws below stay inside these ranges and needn't reach their ends.
All inputs are finite; a program needn't handle non-finite values. No bound on the sum of `action_mask` on one device may be relied on, other than what follows from the above.
Results may differ from the reference program's by a relative error of at most 0.018.
Values may be sent and summed in bfloat16 or wider, within the bound.
A program may use at most 128 MiB of HBM per device.

```python
import math
import jax
import jax.numpy as jnp
from jax import lax

TOK_CP = 128
HEADS = 16
HD = 128
VIS = 2176
HID = 4096
NBINS = 256
NACT = 7
SEQ = 512
EPISODES = 16
NGROUPS = 2
N_CP = 4


def query_key_pair(key):
    base = jax.random.fold_in(key, 31)
    keys_key, target_key, strength_key = jax.random.split(base, 3)
    key_rows = jnp.clip(jax.random.normal(keys_key, (EPISODES, SEQ, HEADS * HD), jnp.float32), -4.0, 4.0)
    key_heads = key_rows.reshape(EPISODES, SEQ, HEADS, HD)
    targets = jax.random.randint(target_key, (EPISODES, SEQ, HEADS, 1), 0, SEQ)
    pointed = jnp.take_along_axis(key_heads, jnp.broadcast_to(targets, (EPISODES, SEQ, HEADS, HD)), axis=1)
    strength = jnp.exp(jax.random.uniform(strength_key, (EPISODES, SEQ, HEADS, 1), jnp.float32, math.log(2.0), math.log(27.0)))
    query_rows = jnp.clip(strength * pointed, -108.0, 108.0).reshape(EPISODES, SEQ, HEADS * HD)
    return (query_rows, key_rows)


def draw_queries(key, part):
    return query_key_pair(key)[0].astype(jnp.bfloat16)


def draw_keys(key, part):
    return query_key_pair(key)[1].astype(jnp.bfloat16)


def draw_values(key, part):
    base = jax.random.fold_in(key, 59)
    coeff_key, direction_key, noise_key = jax.random.split(base, 3)
    coeff = jnp.clip(jax.random.normal(coeff_key, (EPISODES, SEQ, 1), jnp.float32), -3.0, 3.0)
    direction = jnp.clip(jax.random.normal(direction_key, (EPISODES, 1, HEADS * HD), jnp.float32), -3.0, 3.0)
    noise = 0.8 * jax.random.normal(noise_key, (EPISODES, SEQ, HEADS * HD), jnp.float32)
    return jnp.clip(coeff * direction + noise, -6.0, 6.0).astype(jnp.bfloat16)


def draw_act_embed(key, part):
    base = 0.03 * jnp.clip(jax.random.normal(jax.random.fold_in(key, 47), (NACT, HID), jnp.float32), -5.0, 5.0)
    return base


def with_ends(result, key, least, largest):
    extent = result.shape
    place = [jax.random.randint(jax.random.fold_in(key, axis), (), 0, extent[axis]) for axis in range(len(extent))]
    result = result.at[tuple(place)].set(least)
    longest = extent.index(max(extent))
    place[longest] = (place[longest] + 1) % extent[longest]
    return result.at[tuple(place)].set(largest)


def shard_levels(key, extent, cuts, smallest, largest):
    level, own = 1.0, jax.random.fold_in(key, 6)
    for position, blocks in cuts:
        heights = jnp.exp(jax.random.uniform(jax.random.fold_in(own, position), (blocks,), jnp.float32, smallest / len(cuts), largest / len(cuts)))
        level = level * jnp.repeat(heights, extent[position] // blocks).reshape([-1 if axis == position else 1 for axis in range(len(extent))])
    return level


def bell_draw(own_key, dims, deviation, limit, cuts=(), held_as=jnp.bfloat16):
    values = jax.random.normal(own_key, dims, jnp.float32) * deviation
    if len(cuts) > 0:
        values = shard_levels(own_key, dims, cuts, -0.22, 0.18) * values
    return jnp.clip(values, min=-limit, max=limit).astype(held_as)


def setup_inputs(seed: int = 0) -> dict:
    key_of = jax.random.split(jax.random.key(seed), 13)
    queries = draw_queries(jax.random.fold_in(key_of[12], 71), 0)
    keys = draw_keys(jax.random.fold_in(key_of[12], 71), 0)
    values = draw_values(jax.random.fold_in(key_of[12], 71), 0)
    lengths = with_ends(jax.random.randint(key_of[3], (EPISODES,), TOK_CP * N_CP // 4, TOK_CP * N_CP + 1), jax.random.fold_in(key_of[3], 1), TOK_CP * N_CP // 4, TOK_CP * N_CP).astype(jnp.int32)
    frame_map = bell_draw(key_of[4], (HEADS * HD, VIS), (HEADS * HD) ** -0.5, 0.125)
    proj_weight = bell_draw(key_of[5], (VIS, HID), VIS ** -0.5, 0.125, ((0, 8), (1, 4)))
    head_weight = bell_draw(key_of[6], (HID, NBINS), (HID // 16) ** -0.5, 0.375, ((0, 4),))
    act_embed = draw_act_embed(jax.random.fold_in(key_of[12], 71), 0)
    actions = with_ends(jax.random.randint(key_of[8], (EPISODES, NACT), 0, NBINS), jax.random.fold_in(key_of[8], 1), 0, NBINS - 1).astype(jnp.int32)
    action_mask = with_ends((jax.random.randint(key_of[9], (EPISODES, NACT), 0, 4) < 3).astype(jnp.int32), jax.random.fold_in(key_of[9], 1), 0, 1)
    group_ids = with_ends(jax.random.randint(key_of[10], (EPISODES,), 0, NGROUPS), jax.random.fold_in(key_of[10], 1), 0, NGROUPS - 1).astype(jnp.int32)
    rewards = bell_draw(key_of[11], (EPISODES,), 1.0, 6.0, ((0, 8),), jnp.float32)
    return dict(queries=queries, keys=keys, values=values, lengths=lengths, frame_map=frame_map, proj_weight=proj_weight, head_weight=head_weight, act_embed=act_embed, actions=actions, action_mask=action_mask, group_ids=group_ids, rewards=rewards)


SQRT_HALF = 0.7071067811865476
INV_ROOT_TAU = 0.3989422804014327
NEG_LARGE = -1e+30

def gelu_exact(values_in):
    return 0.5 * values_in * (1.0 + lax.erf(values_in * SQRT_HALF))

def gelu_slope(values_in):
    return 0.5 * (1.0 + lax.erf(values_in * SQRT_HALF)) + values_in * jnp.exp(-0.5 * values_in * values_in) * INV_ROOT_TAU

def attend(query_rows, key_rows, value_rows, length):
    query_heads = query_rows.reshape(SEQ, HEADS, HD).astype(jnp.float32)
    key_heads = key_rows.reshape(SEQ, HEADS, HD).astype(jnp.float32)
    value_heads = value_rows.reshape(SEQ, HEADS, HD).astype(jnp.float32)
    scores = jnp.einsum('ihd,jhd->hij', query_heads, key_heads) / math.sqrt(HD)
    live_keys = jnp.arange(SEQ, dtype=jnp.int32) < length
    scores = jnp.where(live_keys[None, None, :], scores, NEG_LARGE)
    row_max = lax.optimization_barrier(jnp.max(scores, axis=-1, keepdims=True))
    probs = jnp.where(live_keys[None, None, :], jnp.exp(scores - row_max), 0.0)
    row_total = lax.optimization_barrier(jnp.sum(probs, axis=-1))
    weighted = jnp.einsum('hij,jhd->ihd', probs.astype(jnp.bfloat16).astype(jnp.float32), value_heads)
    output = weighted / jnp.transpose(row_total)[:, :, None]
    return output.reshape(SEQ, HEADS * HD).astype(jnp.bfloat16)

def reference(queries, keys, values, lengths, frame_map, proj_weight, head_weight, act_embed, actions, action_mask, group_ids, rewards):
    positions = jnp.arange(SEQ, dtype=jnp.int32)

    def forward(element):
        query_rows, key_rows, value_rows, length = element
        attended = attend(query_rows, key_rows, value_rows, length)
        frames = jnp.dot(attended, frame_map, preferred_element_type=jnp.float32).astype(jnp.bfloat16)
        hidden = gelu_exact(jnp.dot(frames, proj_weight, preferred_element_type=jnp.float32))
        token_mask = (positions < length).astype(jnp.float32)
        pooled = lax.optimization_barrier(jnp.sum(token_mask[:, None] * hidden, axis=0)) / length.astype(jnp.float32)
        return (frames, pooled)
    frames, pooled = lax.map(forward, (queries, keys, values, lengths))
    sum_input = pooled[:, None, :] + act_embed[None, :, :]
    head_input = sum_input.astype(jnp.bfloat16).reshape(EPISODES * NACT, HID)
    logits = jnp.dot(head_input, head_weight, preferred_element_type=jnp.float32)
    log_all = jax.nn.log_softmax(logits, axis=-1)
    bin_ids = jnp.arange(NBINS, dtype=jnp.int32)
    picked = (actions.reshape(-1)[:, None] == bin_ids[None, :]).astype(jnp.float32)
    logprobs = lax.optimization_barrier(jnp.sum(picked * log_all, axis=-1)).reshape(EPISODES, NACT)
    membership = (group_ids[:, None] == jnp.arange(NGROUPS, dtype=jnp.int32)[None, :]).astype(jnp.float32)
    group_sizes = lax.optimization_barrier(jnp.sum(membership, axis=0))
    reward_sums = lax.optimization_barrier(jnp.sum(membership * rewards[:, None], axis=0))
    squares = lax.optimization_barrier(jnp.sum(membership * (rewards * rewards)[:, None], axis=0))
    size_floor = jnp.maximum(group_sizes, 1.0)
    group_mean = reward_sums / size_floor
    variance = squares / size_floor - group_mean * group_mean
    group_scale = jnp.sqrt(jnp.maximum(variance, 1.0))
    advantage = (rewards - lax.optimization_barrier(jnp.sum(membership * group_mean[None, :], axis=1))) / lax.optimization_barrier(jnp.sum(membership * group_scale[None, :], axis=1))
    masked = action_mask.astype(jnp.float32)
    mask_total = jnp.maximum(jnp.sum(masked), 1.0)
    loss_weight = (-masked * advantage[:, None] / mask_total).reshape(-1)
    logit_grad = (loss_weight[:, None] * (picked - jnp.exp(log_all))).astype(jnp.bfloat16)
    grad_head = jnp.dot(jnp.transpose(head_input), logit_grad, preferred_element_type=jnp.float32).astype(jnp.bfloat16)
    pool_grad = lax.optimization_barrier(jnp.sum(jnp.dot(logit_grad, jnp.transpose(head_weight), preferred_element_type=jnp.float32).reshape(EPISODES, NACT, HID), axis=1))

    def accumulate(running, element):
        frame_rows, length, pull = element
        pre_act = jnp.dot(frame_rows, proj_weight, preferred_element_type=jnp.float32)
        token_mask = (positions < length).astype(jnp.float32) / length.astype(jnp.float32)
        act_grad = (token_mask[:, None] * pull[None, :] * gelu_slope(pre_act)).astype(jnp.bfloat16)
        return (running + jnp.dot(jnp.transpose(frame_rows), act_grad, preferred_element_type=jnp.float32), None)
    start_grad = jnp.zeros((VIS, HID), jnp.float32)
    grad_proj, _ = lax.scan(accumulate, start_grad, (frames, lengths, pool_grad))
    return (logprobs, grad_proj.astype(jnp.bfloat16), grad_head)
```

```python
import math

import jax
import jax.numpy as jnp
from jax import lax
from jax.experimental import pallas as pl
from jax.experimental.pallas import tpu as pltpu
from jax.sharding import PartitionSpec as P

HD = 128
ON_MESH = pl.DeviceIdType.MESH

SQRT_HALF = 0.7071067811865476
INV_ROOT_TAU = 0.3989422804014327
NEG_LARGE = -1e30


def remote(source, target, send_sem, recv_sem, where):
    return pltpu.make_async_remote_copy(
        src_ref=source,
        dst_ref=target,
        send_sem=send_sem,
        recv_sem=recv_sem,
        device_id=where,
        device_id_type=ON_MESH,
    )


def greet(peers):
    barrier = pltpu.get_barrier_semaphore()
    for where in peers:
        pl.semaphore_signal(barrier, inc=1, device_id=where, device_id_type=ON_MESH)
    pl.semaphore_wait(barrier, len(peers))


def step_kernel(
    n_cp,
    n_out,
    group_count,
    parts,
    length_ref,
    action_ref,
    mask_ref,
    id_ref,
    reward_ref,
    query_ref,
    key_ref,
    value_ref,
    map_ref,
    shard_ref,
    embed_hbm,
    weight_hbm,
    logprob_ref,
    out_ref,
    grad_head_ref,
    heads_all,
    blocks,
    map_held,
    columns_ref,
    frames_ref,
    slope_ref,
    moments,
    pooled_ref,
    embed_ref,
    weight_ref,
    head_rows,
    head_ref,
    logits_send,
    logits_all,
    stats_send,
    stats_all,
    head_all,
    grad_send,
    grad_all,
    pulls,
    pair_send,
    pair_recv,
    line_send,
    line_recv,
    local_sems,
    swap_send,
    swap_recv,
    block_send,
    block_recv,
    shard_send,
    shard_recv,
    pass_send,
    pass_recv,
    logits_sems,
    stats_sems,
    head_sems,
    grad_sems,
    pair_sems,
    line_sends,
    line_recvs,
):
    episodes, tokens, _ = query_ref.shape
    action_count = action_ref.shape[1]
    width = blocks.shape[2]
    seq = tokens * n_cp
    features, units = columns_ref.shape
    chunk = shard_ref.shape[0]
    rows, bins = logits_send.shape
    span = pair_send.shape[3]
    n_grp = 2 * n_out
    last = n_out - 1
    me, group = lax.axis_index("cp"), lax.axis_index("grp")
    place, core = group // 2, lax.rem(group, 2)
    sibling = 2 * place + 1 - core
    above, below = (me, lax.rem(group + 2, n_grp)), (me, lax.rem(group + n_grp - 2, n_grp))
    square = n_cp == 4
    if square:
        row_peer = me + 1 - 2 * lax.rem(me, 2)
        col_peer = lax.rem(me + 2, 4)
        far_peer = lax.rem(row_peer + 2, 4)
        peers = [far_peer, row_peer, col_peer]
    else:
        peers = [lax.rem(me + step, n_cp) for step in range(1, n_cp)]
    lines = [2 * lax.rem(place + step, n_out) + core for step in range(1, n_out)]
    peers_g = [lax.rem(group + step, n_grp) for step in range(1, n_grp)]

    def shard_rows(owner):
        return columns_ref.at[pl.ds(pl.multiple_of(owner * chunk, 8), chunk), :]

    def my_copy(tensor, source, episode):
        return pltpu.make_async_copy(
            source.at[episode, :, pl.ds(pl.multiple_of(me * width, 128), width)],
            heads_all.at[tensor, episode, pl.ds(pl.multiple_of(me * tokens, 8), tokens), :],
            local_sems.at[4 + tensor * episodes + episode],
        )

    def swap_copy(tensor, source, episode, step, owner, peer):
        return remote(
            source.at[episode, :, pl.ds(pl.multiple_of(peer * width, 128), width)],
            heads_all.at[tensor, episode, pl.ds(pl.multiple_of(owner * tokens, 8), tokens), :],
            swap_send.at[tensor, episode, step],
            swap_recv.at[tensor, episode, owner],
            (peer, group),
        )

    def shard_copy(step, owner, peer):
        return remote(shard_ref, shard_rows(owner), shard_send.at[step], shard_recv.at[owner], (me, peer))

    def pass_copy(step, owner, source):
        return remote(source, shard_rows(owner), pass_send.at[step], pass_recv.at[owner], (me, sibling))

    def to_all(send, everyone, sems, step, owner, where):
        return remote(send, everyone.at[owner], sems.at[0, step], sems.at[1, owner], where)

    sources = (query_ref, key_ref, value_ref)
    map_copy = pltpu.make_async_copy(map_ref, map_held, local_sems.at[0])
    keep_copy = pltpu.make_async_copy(shard_ref, shard_rows(group), local_sems.at[1])
    embed_copy = pltpu.make_async_copy(embed_hbm, embed_ref, local_sems.at[2])
    weight_copy = pltpu.make_async_copy(weight_hbm, weight_ref, local_sems.at[3])

    greet([(peer, group) for peer in peers] + [(me, peer) for peer in peers_g])
    for episode in range(episodes):
        for tensor, source in enumerate(sources):
            for step, peer in enumerate(peers):
                swap_copy(tensor, source, episode, step, me, peer).start()
            my_copy(tensor, source, episode).start()
    for step, peer in reversed(list(enumerate(lines))):
        shard_copy(step, group, peer).start()
    pass_copy(n_out - 1, group, shard_ref).start()
    map_copy.start()
    keep_copy.start()
    embed_copy.start()
    weight_copy.start()

    lane = lax.broadcasted_iota(jnp.int32, (8, 128), 1)
    stats = jnp.zeros((8, 128), jnp.float32)
    for episode in range(episodes):
        reward, member = reward_ref[episode], id_ref[episode]
        stats = stats + jnp.where(lane == member, reward, 0.0)
        stats = stats + jnp.where(lane == group_count + member, reward * reward, 0.0)
        stats = stats + jnp.where(lane == 2 * group_count + member, 1.0, 0.0)
        for action in range(action_count):
            valid = mask_ref[episode, action].astype(jnp.float32)
            stats = stats + jnp.where(lane == 3 * group_count, valid, 0.0)
    stats_send[...] = stats
    stats_all[group] = stats
    for step, peer in enumerate(peers_g):
        to_all(stats_send, stats_all, stats_sems, step, group, (me, peer)).start()

    pooled_ref[...] = jnp.zeros_like(pooled_ref)
    head_rows[...] = jnp.zeros_like(head_rows)

    tall_query = min(seq, 256)

    def attend(episode):
        live = lax.broadcasted_iota(jnp.int32, (tall_query, seq), 1) < length_ref[episode]

        def one_head(head, carry):
            at = pl.ds(pl.multiple_of(head * HD, HD), HD)
            key_head = heads_all[1, episode, :, at]
            value_head = heads_all[2, episode, :, at]
            for first in range(0, seq, tall_query):
                query_head = heads_all[0, episode, first : first + tall_query, at]
                scores = lax.dot_general(
                    query_head, key_head, (((1,), (1,)), ((), ())), preferred_element_type=jnp.float32
                )
                scores = jnp.where(live, scores * (1.0 / math.sqrt(HD)), NEG_LARGE)
                probs = jnp.exp(scores - jnp.max(scores, axis=1, keepdims=True))
                row_total = jnp.sum(probs, axis=1, keepdims=True)
                weighted = jnp.dot(probs.astype(jnp.bfloat16), value_head, preferred_element_type=jnp.float32)
                blocks[me, episode * seq + first : episode * seq + first + tall_query, at] = (
                    weighted / row_total
                ).astype(jnp.bfloat16)
            return carry

        lax.fori_loop(0, width // HD, one_head, 0)

    per_band = units // 256
    tiles, spare = divmod(features, 256)
    bands = -(-(tiles + 1) // max(per_band, 1))
    staged = square and episodes == 2 and per_band > 0 and bands * seq <= features and seq % 128 == 0

    def add_frames(episode, first, tall, owners, opens, closes):
        def one_tile(index, at, lanes):
            part = None
            for owner in owners:
                depth = pl.ds(pl.multiple_of(owner * width, 128), width)
                term = jnp.dot(
                    blocks[owner, episode * seq + first : episode * seq + first + tall, :],
                    map_held[depth, at],
                    preferred_element_type=jnp.float32,
                )
                part = term if part is None else part + term
            if not (opens and closes):
                across = lax.rem(index, per_band) * 256
                down = lax.div(index, per_band) * seq + first
                if not isinstance(index, int):
                    across, down = pl.multiple_of(across, 256), pl.multiple_of(down, 8)
                held = (episode, pl.ds(down, tall), pl.ds(across, lanes))
                if not opens:
                    part = part + moments[held]
            if closes:
                frames_ref[episode, first : first + tall, at] = part.astype(jnp.bfloat16)
            else:
                moments[held] = part

        def step(index, carry):
            one_tile(index, pl.ds(pl.multiple_of(index * 256, 256), 256), 256)
            return carry

        lax.fori_loop(0, tiles, step, 0)
        if spare:
            one_tile(jnp.int32(tiles), pl.ds(tiles * 256, spare), spare)

    wide = min(units, 256)

    def activate(episode, first, tall):
        length = jnp.full((tall, 1), length_ref[episode], jnp.int32)
        kept = lax.broadcasted_iota(jnp.int32, (tall, 1), 0) + first < length
        scale = jnp.where(kept, 1.0 / length.astype(jnp.float32), 0.0)

        def step(index, carry):
            at = pl.ds(pl.multiple_of(index * wide, 128), wide)
            pre_act = jnp.dot(
                frames_ref[episode, first : first + tall, :],
                columns_ref[:, at],
                preferred_element_type=jnp.float32,
            )
            below_it = 0.5 * (1.0 + lax.erf(pre_act * SQRT_HALF))
            pooled_ref[episode : episode + 1, at] += jnp.sum(
                scale * (pre_act * below_it), axis=0, keepdims=True
            )
            slope = below_it + pre_act * jnp.exp(-0.5 * pre_act * pre_act) * INV_ROOT_TAU
            slope_ref[episode, first : first + tall, at] = (scale * slope).astype(jnp.bfloat16)
            return carry

        lax.fori_loop(0, units // wide, step, 0)

    def find_moments(episode):
        def one_tile(at):
            moments[episode, at, :] = lax.dot_general(
                frames_ref[episode, :, at],
                slope_ref[episode],
                (((0,), (0,)), ((), ())),
                preferred_element_type=jnp.float32,
            )

        def step(index, carry):
            one_tile(pl.ds(pl.multiple_of(index * 256, 256), 256))
            return carry

        lax.fori_loop(0, tiles, step, 0)
        if spare:
            one_tile(pl.ds(tiles * 256, spare))

    def wait_heads(episode):
        for tensor, source in enumerate(sources):
            my_copy(tensor, source, episode).wait()
            for peer in peers:
                swap_copy(tensor, source, episode, 0, peer, peer).wait_recv()

    def forward_shards():
        for step, peer in enumerate(lines):
            shard_copy(step, peer, peer).wait_recv()
            pass_copy(step, peer, columns_ref.at[pl.ds(pl.multiple_of(peer * chunk, 8), chunk), :]).start()

    def wait_columns():
        for step, peer in enumerate(lines):
            pass_copy(step, peer + 1 - 2 * core, shard_rows(peer)).wait_recv()
        pass_copy(n_out - 1, sibling, shard_ref).wait_recv()
        keep_copy.wait()

    def block_copy(strip, step, owner, peer, at, part):
        held = blocks.at[owner, pl.ds(*at), :]
        return remote(held, held, block_send.at[strip, step], block_recv.at[strip, owner, part], (peer, group))

    if staged:
        strips = [(0, first, seq // 2) for first in range(0, seq, seq // 2)]
        strips += [(1, first, seq // 4) for first in range(0, seq, seq // 4)]

        def whole_of(strip):
            episode, first, tall = strips[strip]
            return episode * seq + first, tall

        def half_of(strip, which):
            start, tall = whole_of(strip)
            return start + which * (tall // 2), tall // 2

        def own(strip):
            block_copy(strip, 0, me, row_peer, whole_of(strip), 0).start()
            block_copy(strip, 1, me, col_peer, whole_of(strip), 0).start()

        def forward(strip):
            block_copy(strip, 0, row_peer, row_peer, whole_of(strip), 0).wait_recv()
            block_copy(strip, 2, row_peer, col_peer, half_of(strip, 0), 0).start()
            block_copy(strip, 1, col_peer, col_peer, whole_of(strip), 0).wait_recv()
            block_copy(strip, 3, col_peer, row_peer, half_of(strip, 1), 1).start()

        def add_near(strip):
            add_frames(*strips[strip], [row_peer, col_peer], False, False)

        def add_far(strip):
            block_copy(strip, 2, far_peer, col_peer, half_of(strip, 0), 0).wait_recv()
            block_copy(strip, 3, far_peer, row_peer, half_of(strip, 1), 1).wait_recv()
            add_frames(*strips[strip], [far_peer], False, True)

        wait_heads(0)
        attend(0)
        own(0)
        own(1)
        map_copy.wait()
        add_frames(0, 0, seq, [me], True, False)
        wait_heads(1)
        attend(1)
        add_frames(1, 0, seq, [me], True, False)
        forward(0)
        add_near(0)
        forward(1)
        own(2)
        own(3)
        add_near(1)
        forward_shards()
        add_far(0)
        add_far(1)
        wait_columns()
        activate(*strips[0])
        forward(2)
        own(4)
        add_near(2)
        activate(*strips[1])
        forward(3)
        own(5)
        add_near(3)
        find_moments(0)
        add_far(2)
        activate(*strips[2])
        forward(4)
        add_near(4)
        add_far(3)
        forward(5)
        add_near(5)
        activate(*strips[3])
        add_far(4)
        activate(*strips[4])
        add_far(5)
        activate(*strips[5])
    else:
        tall = min(seq, 512)
        for episode in range(episodes):
            wait_heads(episode)
            attend(episode)
            for step, peer in enumerate(peers):
                block_copy(episode, step, me, peer, (episode * seq, seq), 0).start()
        map_copy.wait()
        forward_shards()
        wait_columns()
        for episode in range(episodes):
            for step, peer in enumerate(peers):
                block_copy(episode, step, peer, peer, (episode * seq, seq), 0).wait_recv()
            for first in range(0, seq, tall):
                add_frames(episode, first, tall, [me] + peers, True, True)
                activate(episode, first, tall)
            if episode < episodes - 1:
                find_moments(episode)

    embed_copy.wait()
    weight_copy.wait()
    for episode in range(episodes):
        head_rows[episode * action_count : (episode + 1) * action_count, :] = (
            pooled_ref[episode : episode + 1, :] + embed_ref[...]
        )
    head_ref[...] = head_rows[...].astype(jnp.bfloat16)
    partial = jnp.dot(head_ref[...], weight_ref[...], preferred_element_type=jnp.float32)
    logits_send[...] = partial
    logits_all[me] = partial
    for step, peer in enumerate(peers):
        to_all(logits_send, logits_all, logits_sems, step, me, (peer, group)).start()
    head_all[group] = head_ref[...]
    for step, peer in enumerate(peers_g):
        to_all(head_ref, head_all, head_sems, step, group, (me, peer)).start()

    find_moments(episodes - 1)

    for peer in peers_g:
        to_all(stats_send, stats_all, stats_sems, 0, peer, (me, peer)).wait_recv()
    stats = jnp.sum(stats_all[...], axis=0)[0:1]
    lane = lane[0:1]

    def entry(index):
        return jnp.sum(jnp.where(lane == index, stats, 0.0), axis=1, keepdims=True)

    mask_total = jnp.maximum(entry(3 * group_count), 1.0)
    row = lax.broadcasted_iota(jnp.int32, (rows, 1), 0)
    chosen = jnp.zeros((rows, 1), jnp.int32)
    loss_weight = jnp.zeros((rows, 1), jnp.float32)
    for episode in range(episodes):
        member = id_ref[episode]
        size = jnp.maximum(entry(2 * group_count + member), 1.0)
        mean = entry(member) / size
        variance = entry(group_count + member) / size - mean * mean
        advantage = (reward_ref[episode] - mean) / jnp.sqrt(jnp.maximum(variance, 1.0))
        for action in range(action_count):
            here = row == episode * action_count + action
            chosen = jnp.where(here, action_ref[episode, action], chosen)
            valid = mask_ref[episode, action].astype(jnp.float32)
            loss_weight = jnp.where(here, -valid * advantage / mask_total, loss_weight)
    picked = (lax.broadcasted_iota(jnp.int32, (rows, bins), 1) == chosen).astype(jnp.float32)

    for peer in peers:
        to_all(logits_send, logits_all, logits_sems, 0, peer, (peer, group)).wait_recv()
    logits = logits_all[0]
    for slot in range(1, n_cp):
        logits = logits + logits_all[slot]
    shifted = logits - jnp.max(logits, axis=1, keepdims=True)
    log_all = shifted - jnp.log(jnp.sum(jnp.exp(shifted), axis=1, keepdims=True))
    logprob = jnp.sum(picked * log_all, axis=1, keepdims=True)
    logit_grad = (loss_weight * (picked - jnp.exp(log_all))).astype(jnp.bfloat16)
    pull_back = lax.dot_general(
        logit_grad, weight_ref[...], (((1,), (1,)), ((), ())), preferred_element_type=jnp.float32
    )
    for episode in range(episodes):
        mine = jnp.logical_and(row >= episode * action_count, row < (episode + 1) * action_count)
        pulls[episode : episode + 1, :] = jnp.sum(jnp.where(mine, pull_back, 0.0), axis=0, keepdims=True)
    grad_send[...] = logit_grad
    grad_all[group] = logit_grad

    block = 16 if chunk % 16 == 0 else 8

    def fill(target, slot, part, terms):
        at = pl.ds(pl.multiple_of(part * span, 128), span)
        scales = [pulls[episode : episode + 1, at] for episode in range(episodes)]

        def some(index, carry):
            here = pl.ds(pl.multiple_of(index * block, block), block)
            down = pl.ds(pl.multiple_of(slot * chunk + index * block, 8), block)
            total = moments[0, down, at] * scales[0]
            for episode in range(1, episodes):
                total = total + moments[episode, down, at] * scales[episode]
            for term in terms:
                total = total + term[here, :].astype(jnp.float32)
            target[here, :] = total.astype(jnp.bfloat16)
            return carry

        lax.fori_loop(0, chunk // block, some, 0)

    def pair_copy(target, part):
        return remote(
            pair_send.at[target, part],
            pair_recv.at[target, part],
            pair_sems.at[0, target, part],
            pair_sems.at[1, target, part],
            (me, sibling),
        )

    def line_copy(slot, part, where):
        return remote(
            line_send.at[slot, part],
            line_recv.at[slot, part],
            line_sends.at[slot, part],
            line_recvs.at[slot, part],
            where,
        )

    def up_copy(target, part):
        return line_copy(target + 1, part, above)

    def down_copy(target, part):
        return line_copy(target, part, below)

    def give(target, part):
        fill(pair_send.at[target, part], 2 * target + 1 - core, part, [])
        pair_copy(target, part).start()

    def pass_on(target, part, slot, ends, copy):
        pair_copy(target, part).wait_recv()
        own_part = [pair_recv.at[target, part]]
        goal = line_send.at[slot, part]

        @pl.when(ends)
        def _():
            fill(goal, 2 * target + core, part, own_part)

        @pl.when(jnp.logical_not(ends))
        def _():
            copy(target, part).wait_recv()
            fill(goal, 2 * target + core, part, own_part + [line_recv.at[slot, part]])

        copy(target, part).start()

    steps = last * parts

    def give_at(index):
        time, part = lax.div(index, parts), lax.rem(index, parts)
        early = index < steps

        @pl.when(jnp.logical_and(early, time >= place))
        def _():
            give(last + place - time, part)

        @pl.when(jnp.logical_and(early, time >= last - place))
        def _():
            give(time - last + place, part)

        @pl.when(jnp.logical_not(early))
        def _():
            give(place, index - steps)

    def pass_at(index):
        time, part = lax.div(index, parts), lax.rem(index, parts)

        @pl.when(time >= place)
        def _():
            target = last + place - time
            pass_on(target, part, target + 1, place == 0, up_copy)

        @pl.when(time >= last - place)
        def _():
            target = time - last + place
            pass_on(target, part, target, place == last, down_copy)

    def open_up(index, carry):
        give_at(index)
        return carry

    def go_on(index, carry):
        give_at(index + parts)
        pass_at(index)
        return carry

    lax.fori_loop(0, parts, open_up, 0)
    for step, peer in enumerate(peers_g):
        to_all(grad_send, grad_all, grad_sems, step, group, (me, peer)).start()
    lax.fori_loop(0, steps, go_on, 0)

    cell = lax.broadcasted_iota(jnp.int32, (episodes, action_count), 0) * action_count
    cell = cell + lax.broadcasted_iota(jnp.int32, (episodes, action_count), 1)
    laid = jnp.zeros((episodes, action_count), jnp.float32)
    for index in range(episodes * action_count):
        laid = jnp.where(cell == index, logprob[index : index + 1, :], laid)
    logprob_ref[...] = laid
    for peer in peers_g:
        to_all(head_ref, head_all, head_sems, 0, peer, (me, peer)).wait_recv()
        to_all(grad_send, grad_all, grad_sems, 0, peer, (me, peer)).wait_recv()
    grad_head_ref[...] = lax.dot_general(
        head_all[...].reshape(n_grp * rows, units),
        grad_all[...].reshape(n_grp * rows, bins),
        (((0,), (0,)), ((), ())),
        preferred_element_type=jnp.float32,
    ).astype(jnp.bfloat16)

    for part in range(parts):
        goal = out_ref.at[:, pl.ds(part * span, span)]
        pair_copy(place, part).wait_recv()
        own_part = [pair_recv.at[place, part]]
        rose, fell = line_recv.at[place + 1, part], line_recv.at[place, part]

        @pl.when(place == 0)
        def _():
            down_copy(place, part).wait_recv()
            fill(goal, group, part, own_part + [fell])

        @pl.when(place == last)
        def _():
            up_copy(place, part).wait_recv()
            fill(goal, group, part, own_part + [rose])

        @pl.when(jnp.logical_and(place > 0, place < last))
        def _():
            up_copy(place, part).wait_recv()
            down_copy(place, part).wait_recv()
            fill(goal, group, part, own_part + [rose, fell])

    for target in range(n_out):
        for part in range(parts):
            pair_copy(target, part).wait_send()

            @pl.when(target > place)
            def _():
                up_copy(target, part).wait_send()

            @pl.when(target < place)
            def _():
                down_copy(target, part).wait_send()

    for step, peer in enumerate(peers):
        to_all(logits_send, logits_all, logits_sems, step, me, (peer, group)).wait_send()
    for step, peer in enumerate(peers_g):
        to_all(stats_send, stats_all, stats_sems, step, group, (me, peer)).wait_send()
        to_all(head_ref, head_all, head_sems, step, group, (me, peer)).wait_send()
        to_all(grad_send, grad_all, grad_sems, step, group, (me, peer)).wait_send()
    for episode in range(episodes):
        for tensor, source in enumerate(sources):
            for step, peer in enumerate(peers):
                swap_copy(tensor, source, episode, step, me, peer).wait_send()
    if staged:
        for strip in range(len(strips)):
            block_copy(strip, 0, me, row_peer, whole_of(strip), 0).wait_send()
            block_copy(strip, 1, me, col_peer, whole_of(strip), 0).wait_send()
            block_copy(strip, 2, row_peer, col_peer, half_of(strip, 0), 0).wait_send()
            block_copy(strip, 3, col_peer, row_peer, half_of(strip, 1), 1).wait_send()
    else:
        for episode in range(episodes):
            for step, peer in enumerate(peers):
                block_copy(episode, step, me, peer, (episode * seq, seq), 0).wait_send()
    for step, peer in enumerate(lines):
        shard_copy(step, group, peer).wait_send()
        pass_copy(step, peer, shard_rows(peer)).wait_send()
    pass_copy(n_out - 1, group, shard_ref).wait_send()


def train_step(
    queries,
    keys,
    values,
    lengths,
    frame_map,
    proj_weight,
    head_weight,
    act_embed,
    actions,
    action_mask,
    group_ids,
    rewards,
):
    n_cp, n_grp = lax.axis_size("cp"), lax.axis_size("grp")
    n_out = n_grp // 2
    episodes, tokens, att_width = queries.shape
    group_count = max(1, episodes * n_grp // 8)
    seq, width = tokens * n_cp, att_width // n_cp
    chunk, units = proj_weight.shape
    features = frame_map.shape[1]
    rows, bins = -(-actions.size // 16) * 16, head_weight.shape[1]
    parts = 2
    strips = episodes + 4
    in_smem = pl.BlockSpec(memory_space=pltpu.SMEM)
    in_vmem = pl.BlockSpec(memory_space=pltpu.VMEM)
    anywhere = pl.BlockSpec(memory_space=pl.ANY)
    dma = pltpu.SemaphoreType.DMA
    bf16, f32 = jnp.bfloat16, jnp.float32
    return pl.pallas_call(
        lambda *refs: step_kernel(n_cp, n_out, group_count, parts, *refs),
        out_shape=(
            jax.ShapeDtypeStruct(actions.shape, f32),
            jax.ShapeDtypeStruct((chunk, units), bf16),
            jax.ShapeDtypeStruct((units, bins), bf16),
        ),
        in_specs=[in_smem] * 5 + [anywhere] * 7,
        out_specs=(in_vmem,) * 3,
        scratch_shapes=[
            pltpu.VMEM((3, episodes, seq, width), bf16),
            pltpu.VMEM((n_cp, episodes * seq, width), bf16),
            pltpu.VMEM(frame_map.shape, bf16),
            pltpu.VMEM((n_grp * chunk, units), bf16),
            pltpu.VMEM((episodes, seq, features), bf16),
            pltpu.VMEM((episodes, seq, units), bf16),
            pltpu.VMEM((episodes, features, units), f32),
            pltpu.VMEM((-(-episodes // 8) * 8, units), f32),
            pltpu.VMEM(act_embed.shape, f32),
            pltpu.VMEM(head_weight.shape, bf16),
            pltpu.VMEM((rows, units), f32),
            pltpu.VMEM((rows, units), bf16),
            pltpu.VMEM((rows, bins), f32),
            pltpu.VMEM((n_cp, rows, bins), f32),
            pltpu.VMEM((8, 128), f32),
            pltpu.VMEM((n_grp, 8, 128), f32),
            pltpu.VMEM((n_grp, rows, units), bf16),
            pltpu.VMEM((rows, bins), bf16),
            pltpu.VMEM((n_grp, rows, bins), bf16),
            pltpu.VMEM((-(-episodes // 8) * 8, units), f32),
            pltpu.VMEM((n_out, parts, chunk, units // parts), bf16),
            pltpu.VMEM((n_out, parts, chunk, units // parts), bf16),
            pltpu.VMEM((n_out + 1, parts, chunk, units // parts), bf16),
            pltpu.VMEM((n_out + 1, parts, chunk, units // parts), bf16),
            dma((4 + 3 * episodes,)),
            dma((3, episodes, n_cp)),
            dma((3, episodes, n_cp)),
            dma((strips, max(n_cp, 4))),
            dma((strips, n_cp, 2)),
            dma((n_out,)),
            dma((n_grp,)),
            dma((n_out,)),
            dma((n_grp,)),
            dma((2, n_cp)),
            dma((2, n_grp)),
            dma((2, n_grp)),
            dma((2, n_grp)),
            dma((2, n_out, parts)),
            dma((n_out + 1, parts)),
            dma((n_out + 1, parts)),
        ],
        compiler_params=pltpu.CompilerParams(
            collective_id=1, has_side_effects=True, vmem_limit_bytes=62 * 1024 * 1024
        ),
        name="train_step",
    )(
        lengths,
        actions,
        action_mask,
        group_ids,
        rewards,
        queries,
        keys,
        values,
        frame_map,
        proj_weight,
        act_embed,
        head_weight,
    )


def write_kernel(first, second, third, first_out, second_out, third_out):
    first_out[...] = first[...]
    second_out[...] = second[...]
    third_out[...] = third[...]


def write_out(*results):
    in_vmem = pl.BlockSpec(memory_space=pltpu.VMEM)
    return pl.pallas_call(
        write_kernel,
        out_shape=tuple(jax.ShapeDtypeStruct(result.shape, result.dtype) for result in results),
        in_specs=[in_vmem] * 3,
        out_specs=(in_vmem,) * 3,
        name="write_out",
    )(*results)


def per_device(*arrays):
    return write_out(*train_step(*arrays))


def solution(mesh):
    in_specs = (
        P("grp", "cp", None),
        P("grp", "cp", None),
        P("grp", "cp", None),
        P("grp"),
        P(),
        P("grp", "cp"),
        P("cp", None),
        P(None, "cp"),
        P("grp", None),
        P("grp", None),
        P("grp"),
        P("grp"),
    )
    out_specs = (P("grp", None), P("grp", "cp"), P("cp", None))
    return jax.shard_map(
        per_device, mesh=mesh, in_specs=in_specs, out_specs=out_specs, check_vma=False
    )
```

```python
import math

import jax
import jax.numpy as jnp
from jax import lax
from jax.experimental import pallas as pl
from jax.experimental.pallas import tpu as pltpu
from jax.sharding import PartitionSpec as P

HD = 128
ON_MESH = pl.DeviceIdType.MESH

SQRT_HALF = 0.7071067811865476
INV_ROOT_TAU = 0.3989422804014327
NEG_LARGE = -1e30


def remote(source, target, send_sem, recv_sem, where):
    return pltpu.make_async_remote_copy(
        src_ref=source,
        dst_ref=target,
        send_sem=send_sem,
        recv_sem=recv_sem,
        device_id=where,
        device_id_type=ON_MESH,
    )


def greet(peers):
    barrier = pltpu.get_barrier_semaphore()
    for where in peers:
        pl.semaphore_signal(barrier, inc=1, device_id=where, device_id_type=ON_MESH)
    pl.semaphore_wait(barrier, len(peers))


def step_kernel(
    n_cp,
    n_out,
    group_count,
    parts,
    length_ref,
    action_ref,
    mask_ref,
    id_ref,
    reward_ref,
    query_ref,
    key_ref,
    value_ref,
    map_ref,
    shard_ref,
    embed_hbm,
    weight_hbm,
    logprob_ref,
    out_ref,
    grad_head_ref,
    heads_all,
    blocks,
    map_held,
    columns_ref,
    frames_ref,
    slope_ref,
    moments,
    pooled_ref,
    embed_ref,
    weight_ref,
    head_rows,
    head_ref,
    logits_send,
    logits_all,
    stats_send,
    stats_all,
    head_all,
    grad_send,
    grad_all,
    pulls,
    pair_send,
    pair_recv,
    line_send,
    line_recv,
    local_sems,
    swap_send,
    swap_recv,
    block_send,
    block_recv,
    shard_send,
    shard_recv,
    pass_send,
    pass_recv,
    logits_sems,
    stats_sems,
    head_sems,
    grad_sems,
    pair_sems,
    line_sends,
    line_recvs,
):
    episodes, tokens, _ = query_ref.shape
    action_count = action_ref.shape[1]
    width = blocks.shape[2]
    seq = tokens * n_cp
    features, units = columns_ref.shape
    chunk = shard_ref.shape[0]
    rows, bins = logits_send.shape
    span = pair_send.shape[3]
    n_grp = 2 * n_out
    last = n_out - 1
    me, group = lax.axis_index("cp"), lax.axis_index("grp")
    place, core = group // 2, lax.rem(group, 2)
    sibling = 2 * place + 1 - core
    above, below = (me, lax.rem(group + 2, n_grp)), (me, lax.rem(group + n_grp - 2, n_grp))
    square = n_cp == 4
    if square:
        row_peer = me + 1 - 2 * lax.rem(me, 2)
        col_peer = lax.rem(me + 2, 4)
        far_peer = lax.rem(row_peer + 2, 4)
        peers = [far_peer, row_peer, col_peer]
    else:
        peers = [lax.rem(me + step, n_cp) for step in range(1, n_cp)]
    lines = [2 * lax.rem(place + step, n_out) + core for step in range(1, n_out)]
    peers_g = [lax.rem(group + step, n_grp) for step in range(1, n_grp)]

    def shard_rows(owner):
        return columns_ref.at[pl.ds(pl.multiple_of(owner * chunk, 8), chunk), :]

    def my_copy(tensor, source, episode):
        return pltpu.make_async_copy(
            source.at[episode, :, pl.ds(pl.multiple_of(me * width, 128), width)],
            heads_all.at[tensor, episode, pl.ds(pl.multiple_of(me * tokens, 8), tokens), :],
            local_sems.at[4 + tensor * episodes + episode],
        )

    def swap_copy(tensor, source, episode, step, owner, peer):
        return remote(
            source.at[episode, :, pl.ds(pl.multiple_of(peer * width, 128), width)],
            heads_all.at[tensor, episode, pl.ds(pl.multiple_of(owner * tokens, 8), tokens), :],
            swap_send.at[tensor, episode, step],
            swap_recv.at[tensor, episode, owner],
            (peer, group),
        )

    def shard_copy(step, owner, peer):
        return remote(shard_ref, shard_rows(owner), shard_send.at[step], shard_recv.at[owner], (me, peer))

    def pass_copy(step, owner, source):
        return remote(source, shard_rows(owner), pass_send.at[step], pass_recv.at[owner], (me, sibling))

    def to_all(send, everyone, sems, step, owner, where):
        return remote(send, everyone.at[owner], sems.at[0, step], sems.at[1, owner], where)

    sources = (query_ref, key_ref, value_ref)
    map_copy = pltpu.make_async_copy(map_ref, map_held, local_sems.at[0])
    keep_copy = pltpu.make_async_copy(shard_ref, shard_rows(group), local_sems.at[1])
    embed_copy = pltpu.make_async_copy(embed_hbm, embed_ref, local_sems.at[2])
    weight_copy = pltpu.make_async_copy(weight_hbm, weight_ref, local_sems.at[3])

    greet([(peer, group) for peer in peers] + [(me, peer) for peer in peers_g])
    for episode in range(episodes):
        for tensor, source in enumerate(sources):
            for step, peer in enumerate(peers):
                swap_copy(tensor, source, episode, step, me, peer).start()
            my_copy(tensor, source, episode).start()
    for step, peer in reversed(list(enumerate(lines))):
        shard_copy(step, group, peer).start()
    pass_copy(n_out - 1, group, shard_ref).start()
    map_copy.start()
    keep_copy.start()
    embed_copy.start()
    weight_copy.start()

    lane = lax.broadcasted_iota(jnp.int32, (8, 128), 1)
    stats = jnp.zeros((8, 128), jnp.float32)
    for episode in range(episodes):
        reward, member = reward_ref[episode], id_ref[episode]
        stats = stats + jnp.where(lane == member, reward, 0.0)
        stats = stats + jnp.where(lane == group_count + member, reward * reward, 0.0)
        stats = stats + jnp.where(lane == 2 * group_count + member, 1.0, 0.0)
        for action in range(action_count):
            valid = mask_ref[episode, action].astype(jnp.float32)
            stats = stats + jnp.where(lane == 3 * group_count, valid, 0.0)
    stats_send[...] = stats
    stats_all[group] = stats
    for step, peer in enumerate(peers_g):
        to_all(stats_send, stats_all, stats_sems, step, group, (me, peer)).start()

    pooled_ref[...] = jnp.zeros_like(pooled_ref)
    head_rows[...] = jnp.zeros_like(head_rows)

    tall_query = min(seq, 256)

    def attend(episode):
        live = lax.broadcasted_iota(jnp.int32, (tall_query, seq), 1) < length_ref[episode]

        def one_head(head, carry):
            at = pl.ds(pl.multiple_of(head * HD, HD), HD)
            key_head = heads_all[1, episode, :, at]
            value_head = heads_all[2, episode, :, at]
            for first in range(0, seq, tall_query):
                query_head = heads_all[0, episode, first : first + tall_query, at]
                scores = lax.dot_general(
                    query_head, key_head, (((1,), (1,)), ((), ())), preferred_element_type=jnp.float32
                )
                scores = jnp.where(live, scores * (1.0 / math.sqrt(HD)), NEG_LARGE)
                probs = jnp.exp(scores - jnp.max(scores, axis=1, keepdims=True))
                row_total = jnp.sum(probs, axis=1, keepdims=True)
                weighted = jnp.dot(probs.astype(jnp.bfloat16), value_head, preferred_element_type=jnp.float32)
                blocks[me, episode * seq + first : episode * seq + first + tall_query, at] = (
                    weighted / row_total
                ).astype(jnp.bfloat16)
            return carry

        lax.fori_loop(0, width // HD, one_head, 0)

    tile = min(units, 512)
    per_band = units // tile
    bands = -(-features // (tile * per_band))
    staged = square and episodes == 2 and bands * seq <= features and seq % 128 == 0

    def add_frames(episode, first, tall, owners, opens, closes):
        for index, left in enumerate(range(0, features, tile)):
            lanes = min(tile, features - left)
            part = None
            for owner in owners:
                term = jnp.dot(
                    blocks[owner, episode * seq + first : episode * seq + first + tall, :],
                    map_held[pl.ds(pl.multiple_of(owner * width, 128), width), left : left + lanes],
                    preferred_element_type=jnp.float32,
                )
                part = term if part is None else part + term
            down, across = index // per_band * seq + first, index % per_band * tile
            held = (episode, slice(down, down + tall), slice(across, across + lanes))
            if not opens:
                part = part + moments[held]
            if closes:
                frames_ref[episode, first : first + tall, left : left + lanes] = part.astype(jnp.bfloat16)
            else:
                moments[held] = part

    def activate(episode, first, tall):
        length = jnp.full((tall, 1), length_ref[episode], jnp.int32)
        kept = lax.broadcasted_iota(jnp.int32, (tall, 1), 0) + first < length
        scale = jnp.where(kept, 1.0 / length.astype(jnp.float32), 0.0)
        for left in range(0, units, tile):
            at = slice(left, left + tile)
            pre_act = jnp.dot(
                frames_ref[episode, first : first + tall, :],
                columns_ref[:, at],
                preferred_element_type=jnp.float32,
            )
            below_it = 0.5 * (1.0 + lax.erf(pre_act * SQRT_HALF))
            pooled_ref[episode : episode + 1, at] += jnp.sum(
                scale * (pre_act * below_it), axis=0, keepdims=True
            )
            slope = below_it + pre_act * jnp.exp(-0.5 * pre_act * pre_act) * INV_ROOT_TAU
            slope_ref[episode, first : first + tall, at] = (scale * slope).astype(jnp.bfloat16)

    def find_moments(episode):
        for left in range(0, features, 256):
            at = slice(left, min(left + 256, features))
            moments[episode, at, :] = lax.dot_general(
                frames_ref[episode, :, at],
                slope_ref[episode],
                (((0,), (0,)), ((), ())),
                preferred_element_type=jnp.float32,
            )

    def wait_heads(episode):
        for tensor, source in enumerate(sources):
            my_copy(tensor, source, episode).wait()
            for peer in peers:
                swap_copy(tensor, source, episode, 0, peer, peer).wait_recv()

    def forward_shards():
        for step, peer in enumerate(lines):
            shard_copy(step, peer, peer).wait_recv()
            pass_copy(step, peer, columns_ref.at[pl.ds(pl.multiple_of(peer * chunk, 8), chunk), :]).start()

    def wait_columns():
        for step, peer in enumerate(lines):
            pass_copy(step, peer + 1 - 2 * core, shard_rows(peer)).wait_recv()
        pass_copy(n_out - 1, sibling, shard_ref).wait_recv()
        keep_copy.wait()

    def block_copy(strip, step, owner, peer, at, part):
        held = blocks.at[owner, pl.ds(*at), :]
        return remote(held, held, block_send.at[strip, step], block_recv.at[strip, owner, part], (peer, group))

    if staged:
        strips = [(0, first, seq // 2) for first in range(0, seq, seq // 2)]
        strips += [(1, first, seq // 4) for first in range(0, seq, seq // 4)]

        def whole_of(strip):
            episode, first, tall = strips[strip]
            return episode * seq + first, tall

        def half_of(strip, which):
            start, tall = whole_of(strip)
            return start + which * (tall // 2), tall // 2

        def own(strip):
            block_copy(strip, 0, me, row_peer, whole_of(strip), 0).start()
            block_copy(strip, 1, me, col_peer, whole_of(strip), 0).start()

        def forward(strip):
            block_copy(strip, 0, row_peer, row_peer, whole_of(strip), 0).wait_recv()
            block_copy(strip, 2, row_peer, col_peer, half_of(strip, 0), 0).start()
            block_copy(strip, 1, col_peer, col_peer, whole_of(strip), 0).wait_recv()
            block_copy(strip, 3, col_peer, row_peer, half_of(strip, 1), 1).start()

        def add_near(strip):
            add_frames(*strips[strip], [me, row_peer, col_peer], True, False)

        def add_far(strip):
            block_copy(strip, 2, far_peer, col_peer, half_of(strip, 0), 0).wait_recv()
            block_copy(strip, 3, far_peer, row_peer, half_of(strip, 1), 1).wait_recv()
            add_frames(*strips[strip], [far_peer], False, True)

        wait_heads(0)
        attend(0)
        own(0)
        own(1)
        wait_heads(1)
        attend(1)
        map_copy.wait()
        forward(0)
        add_near(0)
        forward(1)
        own(2)
        own(3)
        add_near(1)
        forward_shards()
        add_far(0)
        add_far(1)
        wait_columns()
        activate(*strips[0])
        forward(2)
        own(4)
        add_near(2)
        activate(*strips[1])
        forward(3)
        own(5)
        add_near(3)
        add_far(2)
        activate(*strips[2])
        forward(4)
        add_near(4)
        add_far(3)
        activate(*strips[3])
        find_moments(0)
        forward(5)
        add_near(5)
        add_far(4)
        activate(*strips[4])
        add_far(5)
        activate(*strips[5])
    else:
        tall = min(seq, 128)
        for episode in range(episodes):
            wait_heads(episode)
            attend(episode)
            for step, peer in enumerate(peers):
                block_copy(episode, step, me, peer, (episode * seq, seq), 0).start()
        map_copy.wait()
        forward_shards()
        wait_columns()
        for episode in range(episodes):
            for step, peer in enumerate(peers):
                block_copy(episode, step, peer, peer, (episode * seq, seq), 0).wait_recv()
            for first in range(0, seq, tall):
                add_frames(episode, first, tall, [me] + peers, True, True)
                activate(episode, first, tall)
            if episode < episodes - 1:
                find_moments(episode)

    embed_copy.wait()
    weight_copy.wait()
    for episode in range(episodes):
        head_rows[episode * action_count : (episode + 1) * action_count, :] = (
            pooled_ref[episode : episode + 1, :] + embed_ref[...]
        )
    head_ref[...] = head_rows[...].astype(jnp.bfloat16)
    partial = jnp.dot(head_ref[...], weight_ref[...], preferred_element_type=jnp.float32)
    logits_send[...] = partial
    logits_all[me] = partial
    for step, peer in enumerate(peers):
        to_all(logits_send, logits_all, logits_sems, step, me, (peer, group)).start()
    head_all[group] = head_ref[...]
    for step, peer in enumerate(peers_g):
        to_all(head_ref, head_all, head_sems, step, group, (me, peer)).start()

    find_moments(episodes - 1)

    for peer in peers_g:
        to_all(stats_send, stats_all, stats_sems, 0, peer, (me, peer)).wait_recv()
    stats = jnp.sum(stats_all[...], axis=0)[0:1]
    lane = lane[0:1]

    def entry(index):
        return jnp.sum(jnp.where(lane == index, stats, 0.0), axis=1, keepdims=True)

    mask_total = jnp.maximum(entry(3 * group_count), 1.0)
    row = lax.broadcasted_iota(jnp.int32, (rows, 1), 0)
    chosen = jnp.zeros((rows, 1), jnp.int32)
    loss_weight = jnp.zeros((rows, 1), jnp.float32)
    for episode in range(episodes):
        member = id_ref[episode]
        size = jnp.maximum(entry(2 * group_count + member), 1.0)
        mean = entry(member) / size
        variance = entry(group_count + member) / size - mean * mean
        advantage = (reward_ref[episode] - mean) / jnp.sqrt(jnp.maximum(variance, 1.0))
        for action in range(action_count):
            here = row == episode * action_count + action
            chosen = jnp.where(here, action_ref[episode, action], chosen)
            valid = mask_ref[episode, action].astype(jnp.float32)
            loss_weight = jnp.where(here, -valid * advantage / mask_total, loss_weight)
    picked = (lax.broadcasted_iota(jnp.int32, (rows, bins), 1) == chosen).astype(jnp.float32)

    for peer in peers:
        to_all(logits_send, logits_all, logits_sems, 0, peer, (peer, group)).wait_recv()
    logits = logits_all[0]
    for slot in range(1, n_cp):
        logits = logits + logits_all[slot]
    shifted = logits - jnp.max(logits, axis=1, keepdims=True)
    log_all = shifted - jnp.log(jnp.sum(jnp.exp(shifted), axis=1, keepdims=True))
    logprob = jnp.sum(picked * log_all, axis=1, keepdims=True)
    logit_grad = (loss_weight * (picked - jnp.exp(log_all))).astype(jnp.bfloat16)
    pull_back = lax.dot_general(
        logit_grad, weight_ref[...], (((1,), (1,)), ((), ())), preferred_element_type=jnp.float32
    )
    for episode in range(episodes):
        mine = jnp.logical_and(row >= episode * action_count, row < (episode + 1) * action_count)
        pulls[episode : episode + 1, :] = jnp.sum(jnp.where(mine, pull_back, 0.0), axis=0, keepdims=True)
    grad_send[...] = logit_grad
    grad_all[group] = logit_grad

    block = 16 if chunk % 16 == 0 else 8

    def fill(target, slot, part, terms):
        at = pl.ds(pl.multiple_of(part * span, 128), span)
        scales = [pulls[episode : episode + 1, at] for episode in range(episodes)]

        def some(index, carry):
            here = pl.ds(pl.multiple_of(index * block, block), block)
            down = pl.ds(pl.multiple_of(slot * chunk + index * block, 8), block)
            total = moments[0, down, at] * scales[0]
            for episode in range(1, episodes):
                total = total + moments[episode, down, at] * scales[episode]
            for term in terms:
                total = total + term[here, :].astype(jnp.float32)
            target[here, :] = total.astype(jnp.bfloat16)
            return carry

        lax.fori_loop(0, chunk // block, some, 0)

    def pair_copy(target, part):
        return remote(
            pair_send.at[target, part],
            pair_recv.at[target, part],
            pair_sems.at[0, target, part],
            pair_sems.at[1, target, part],
            (me, sibling),
        )

    def line_copy(slot, part, where):
        return remote(
            line_send.at[slot, part],
            line_recv.at[slot, part],
            line_sends.at[slot, part],
            line_recvs.at[slot, part],
            where,
        )

    def up_copy(target, part):
        return line_copy(target + 1, part, above)

    def down_copy(target, part):
        return line_copy(target, part, below)

    def give(target, part):
        fill(pair_send.at[target, part], 2 * target + 1 - core, part, [])
        pair_copy(target, part).start()

    def pass_on(target, part, slot, ends, copy):
        pair_copy(target, part).wait_recv()
        own_part = [pair_recv.at[target, part]]
        goal = line_send.at[slot, part]

        @pl.when(ends)
        def _():
            fill(goal, 2 * target + core, part, own_part)

        @pl.when(jnp.logical_not(ends))
        def _():
            copy(target, part).wait_recv()
            fill(goal, 2 * target + core, part, own_part + [line_recv.at[slot, part]])

        copy(target, part).start()

    steps = last * parts

    def give_at(index):
        time, part = lax.div(index, parts), lax.rem(index, parts)
        early = index < steps

        @pl.when(jnp.logical_and(early, time >= place))
        def _():
            give(last + place - time, part)

        @pl.when(jnp.logical_and(early, time >= last - place))
        def _():
            give(time - last + place, part)

        @pl.when(jnp.logical_not(early))
        def _():
            give(place, index - steps)

    def pass_at(index):
        time, part = lax.div(index, parts), lax.rem(index, parts)

        @pl.when(time >= place)
        def _():
            target = last + place - time
            pass_on(target, part, target + 1, place == 0, up_copy)

        @pl.when(time >= last - place)
        def _():
            target = time - last + place
            pass_on(target, part, target, place == last, down_copy)

    def open_up(index, carry):
        give_at(index)
        return carry

    def go_on(index, carry):
        give_at(index + parts)
        pass_at(index)
        return carry

    lax.fori_loop(0, parts, open_up, 0)
    for step, peer in enumerate(peers_g):
        to_all(grad_send, grad_all, grad_sems, step, group, (me, peer)).start()
    lax.fori_loop(0, steps, go_on, 0)

    cell = lax.broadcasted_iota(jnp.int32, (episodes, action_count), 0) * action_count
    cell = cell + lax.broadcasted_iota(jnp.int32, (episodes, action_count), 1)
    laid = jnp.zeros((episodes, action_count), jnp.float32)
    for index in range(episodes * action_count):
        laid = jnp.where(cell == index, logprob[index : index + 1, :], laid)
    logprob_ref[...] = laid
    for peer in peers_g:
        to_all(head_ref, head_all, head_sems, 0, peer, (me, peer)).wait_recv()
        to_all(grad_send, grad_all, grad_sems, 0, peer, (me, peer)).wait_recv()
    grad_head_ref[...] = lax.dot_general(
        head_all[...].reshape(n_grp * rows, units),
        grad_all[...].reshape(n_grp * rows, bins),
        (((0,), (0,)), ((), ())),
        preferred_element_type=jnp.float32,
    ).astype(jnp.bfloat16)

    for part in range(parts):
        goal = out_ref.at[:, pl.ds(part * span, span)]
        pair_copy(place, part).wait_recv()
        own_part = [pair_recv.at[place, part]]
        rose, fell = line_recv.at[place + 1, part], line_recv.at[place, part]

        @pl.when(place == 0)
        def _():
            down_copy(place, part).wait_recv()
            fill(goal, group, part, own_part + [fell])

        @pl.when(place == last)
        def _():
            up_copy(place, part).wait_recv()
            fill(goal, group, part, own_part + [rose])

        @pl.when(jnp.logical_and(place > 0, place < last))
        def _():
            up_copy(place, part).wait_recv()
            down_copy(place, part).wait_recv()
            fill(goal, group, part, own_part + [rose, fell])

    for target in range(n_out):
        for part in range(parts):
            pair_copy(target, part).wait_send()

            @pl.when(target > place)
            def _():
                up_copy(target, part).wait_send()

            @pl.when(target < place)
            def _():
                down_copy(target, part).wait_send()

    for step, peer in enumerate(peers):
        to_all(logits_send, logits_all, logits_sems, step, me, (peer, group)).wait_send()
    for step, peer in enumerate(peers_g):
        to_all(stats_send, stats_all, stats_sems, step, group, (me, peer)).wait_send()
        to_all(head_ref, head_all, head_sems, step, group, (me, peer)).wait_send()
        to_all(grad_send, grad_all, grad_sems, step, group, (me, peer)).wait_send()
    for episode in range(episodes):
        for tensor, source in enumerate(sources):
            for step, peer in enumerate(peers):
                swap_copy(tensor, source, episode, step, me, peer).wait_send()
    if staged:
        for strip in range(len(strips)):
            block_copy(strip, 0, me, row_peer, whole_of(strip), 0).wait_send()
            block_copy(strip, 1, me, col_peer, whole_of(strip), 0).wait_send()
            block_copy(strip, 2, row_peer, col_peer, half_of(strip, 0), 0).wait_send()
            block_copy(strip, 3, col_peer, row_peer, half_of(strip, 1), 1).wait_send()
    else:
        for episode in range(episodes):
            for step, peer in enumerate(peers):
                block_copy(episode, step, me, peer, (episode * seq, seq), 0).wait_send()
    for step, peer in enumerate(lines):
        shard_copy(step, group, peer).wait_send()
        pass_copy(step, peer, shard_rows(peer)).wait_send()
    pass_copy(n_out - 1, group, shard_ref).wait_send()


def train_step(
    queries,
    keys,
    values,
    lengths,
    frame_map,
    proj_weight,
    head_weight,
    act_embed,
    actions,
    action_mask,
    group_ids,
    rewards,
):
    n_cp, n_grp = lax.axis_size("cp"), lax.axis_size("grp")
    n_out = n_grp // 2
    episodes, tokens, att_width = queries.shape
    group_count = max(1, episodes * n_grp // 8)
    seq, width = tokens * n_cp, att_width // n_cp
    chunk, units = proj_weight.shape
    features = frame_map.shape[1]
    rows, bins = -(-actions.size // 16) * 16, head_weight.shape[1]
    parts = 2
    strips = episodes + 4
    in_smem = pl.BlockSpec(memory_space=pltpu.SMEM)
    in_vmem = pl.BlockSpec(memory_space=pltpu.VMEM)
    anywhere = pl.BlockSpec(memory_space=pl.ANY)
    dma = pltpu.SemaphoreType.DMA
    bf16, f32 = jnp.bfloat16, jnp.float32
    return pl.pallas_call(
        lambda *refs: step_kernel(n_cp, n_out, group_count, parts, *refs),
        out_shape=(
            jax.ShapeDtypeStruct(actions.shape, f32),
            jax.ShapeDtypeStruct((chunk, units), bf16),
            jax.ShapeDtypeStruct((units, bins), bf16),
        ),
        in_specs=[in_smem] * 5 + [anywhere] * 7,
        out_specs=(in_vmem,) * 3,
        scratch_shapes=[
            pltpu.VMEM((3, episodes, seq, width), bf16),
            pltpu.VMEM((n_cp, episodes * seq, width), bf16),
            pltpu.VMEM(frame_map.shape, bf16),
            pltpu.VMEM((n_grp * chunk, units), bf16),
            pltpu.VMEM((episodes, seq, features), bf16),
            pltpu.VMEM((episodes, seq, units), bf16),
            pltpu.VMEM((episodes, features, units), f32),
            pltpu.VMEM((-(-episodes // 8) * 8, units), f32),
            pltpu.VMEM(act_embed.shape, f32),
            pltpu.VMEM(head_weight.shape, bf16),
            pltpu.VMEM((rows, units), f32),
            pltpu.VMEM((rows, units), bf16),
            pltpu.VMEM((rows, bins), f32),
            pltpu.VMEM((n_cp, rows, bins), f32),
            pltpu.VMEM((8, 128), f32),
            pltpu.VMEM((n_grp, 8, 128), f32),
            pltpu.VMEM((n_grp, rows, units), bf16),
            pltpu.VMEM((rows, bins), bf16),
            pltpu.VMEM((n_grp, rows, bins), bf16),
            pltpu.VMEM((-(-episodes // 8) * 8, units), f32),
            pltpu.VMEM((n_out, parts, chunk, units // parts), bf16),
            pltpu.VMEM((n_out, parts, chunk, units // parts), bf16),
            pltpu.VMEM((n_out + 1, parts, chunk, units // parts), bf16),
            pltpu.VMEM((n_out + 1, parts, chunk, units // parts), bf16),
            dma((4 + 3 * episodes,)),
            dma((3, episodes, n_cp)),
            dma((3, episodes, n_cp)),
            dma((strips, max(n_cp, 4))),
            dma((strips, n_cp, 2)),
            dma((n_out,)),
            dma((n_grp,)),
            dma((n_out,)),
            dma((n_grp,)),
            dma((2, n_cp)),
            dma((2, n_grp)),
            dma((2, n_grp)),
            dma((2, n_grp)),
            dma((2, n_out, parts)),
            dma((n_out + 1, parts)),
            dma((n_out + 1, parts)),
        ],
        compiler_params=pltpu.CompilerParams(
            collective_id=1, has_side_effects=True, vmem_limit_bytes=62 * 1024 * 1024
        ),
        name="train_step",
    )(
        lengths,
        actions,
        action_mask,
        group_ids,
        rewards,
        queries,
        keys,
        values,
        frame_map,
        proj_weight,
        act_embed,
        head_weight,
    )


def write_kernel(first, second, third, first_out, second_out, third_out):
    first_out[...] = first[...]
    second_out[...] = second[...]
    third_out[...] = third[...]


def write_out(*results):
    in_vmem = pl.BlockSpec(memory_space=pltpu.VMEM)
    return pl.pallas_call(
        write_kernel,
        out_shape=tuple(jax.ShapeDtypeStruct(result.shape, result.dtype) for result in results),
        in_specs=[in_vmem] * 3,
        out_specs=(in_vmem,) * 3,
        name="write_out",
    )(*results)


def per_device(*arrays):
    return write_out(*train_step(*arrays))


def solution(mesh):
    in_specs = (
        P("grp", "cp", None),
        P("grp", "cp", None),
        P("grp", "cp", None),
        P("grp"),
        P(),
        P("grp", "cp"),
        P("cp", None),
        P(None, "cp"),
        P("grp", None),
        P("grp", None),
        P("grp"),
        P("grp"),
    )
    out_specs = (P("grp", None), P("grp", "cp"), P("cp", None))
    return jax.shard_map(
        per_device, mesh=mesh, in_specs=in_specs, out_specs=out_specs, check_vma=False
    )
```

```python
import math

import jax
import jax.numpy as jnp
from jax import lax
from jax.experimental import pallas as pl
from jax.experimental.pallas import tpu as pltpu
from jax.sharding import PartitionSpec as P

HD = 128
ON_MESH = pl.DeviceIdType.MESH

SQRT_HALF = 0.7071067811865476
INV_ROOT_TAU = 0.3989422804014327
NEG_LARGE = -1e30


def remote(source, target, send_sem, recv_sem, where):
    return pltpu.make_async_remote_copy(
        src_ref=source,
        dst_ref=target,
        send_sem=send_sem,
        recv_sem=recv_sem,
        device_id=where,
        device_id_type=ON_MESH,
    )


def greet(peers):
    barrier = pltpu.get_barrier_semaphore()
    for where in peers:
        pl.semaphore_signal(barrier, inc=1, device_id=where, device_id_type=ON_MESH)
    pl.semaphore_wait(barrier, len(peers))


def step_kernel(
    n_cp,
    n_out,
    group_count,
    parts,
    length_hbm,
    action_hbm,
    mask_hbm,
    id_hbm,
    reward_hbm,
    query_ref,
    key_ref,
    value_ref,
    map_ref,
    shard_ref,
    embed_hbm,
    weight_hbm,
    logprob_hbm,
    out_hbm,
    grad_head_hbm,
    length_ref,
    action_ref,
    mask_ref,
    id_ref,
    reward_ref,
    logprob_ref,
    out_ref,
    grad_head_ref,
    heads_all,
    blocks,
    map_held,
    columns_ref,
    frames_ref,
    slope_ref,
    moments,
    pooled_ref,
    embed_ref,
    weight_ref,
    head_rows,
    head_ref,
    logits_send,
    logits_all,
    stats_send,
    stats_all,
    head_all,
    grad_send,
    grad_all,
    pulls,
    pair_send,
    pair_recv,
    line_send,
    line_recv,
    local_sems,
    swap_send,
    swap_recv,
    block_send,
    block_recv,
    shard_send,
    shard_recv,
    pass_send,
    pass_recv,
    logits_sems,
    stats_sems,
    head_sems,
    grad_sems,
    pair_sems,
    line_sends,
    line_recvs,
    scalar_sems,
    out_sems,
):
    episodes, tokens, _ = query_ref.shape
    action_count = action_ref.shape[1]
    width = blocks.shape[2]
    seq = tokens * n_cp
    features, units = columns_ref.shape
    chunk = shard_ref.shape[0]
    rows, bins = logits_send.shape
    span = pair_send.shape[3]
    n_grp = 2 * n_out
    last = n_out - 1
    me, group = lax.axis_index("cp"), lax.axis_index("grp")
    place, core = group // 2, lax.rem(group, 2)
    sibling = 2 * place + 1 - core
    above, below = (me, lax.rem(group + 2, n_grp)), (me, lax.rem(group + n_grp - 2, n_grp))
    square = n_cp == 4
    if square:
        row_peer = me + 1 - 2 * lax.rem(me, 2)
        col_peer = lax.rem(me + 2, 4)
        far_peer = lax.rem(row_peer + 2, 4)
        peers = [far_peer, row_peer, col_peer]
    else:
        peers = [lax.rem(me + step, n_cp) for step in range(1, n_cp)]
    lines = [2 * lax.rem(place + step, n_out) + core for step in range(1, n_out)]
    peers_g = [lax.rem(group + step, n_grp) for step in range(1, n_grp)]

    def shard_rows(owner):
        return columns_ref.at[pl.ds(pl.multiple_of(owner * chunk, 8), chunk), :]

    def my_copy(tensor, source, episode):
        return pltpu.make_async_copy(
            source.at[episode, :, pl.ds(pl.multiple_of(me * width, 128), width)],
            heads_all.at[tensor, episode, pl.ds(pl.multiple_of(me * tokens, 8), tokens), :],
            local_sems.at[4 + tensor * episodes + episode],
        )

    def swap_copy(tensor, source, episode, step, owner, peer):
        return remote(
            source.at[episode, :, pl.ds(pl.multiple_of(peer * width, 128), width)],
            heads_all.at[tensor, episode, pl.ds(pl.multiple_of(owner * tokens, 8), tokens), :],
            swap_send.at[tensor, episode, step],
            swap_recv.at[tensor, episode, owner],
            (peer, group),
        )

    def shard_copy(step, owner, peer):
        return remote(shard_ref, shard_rows(owner), shard_send.at[step], shard_recv.at[owner], (me, peer))

    def pass_copy(step, owner, source):
        return remote(source, shard_rows(owner), pass_send.at[step], pass_recv.at[owner], (me, sibling))

    def to_all(send, everyone, sems, step, owner, where):
        return remote(send, everyone.at[owner], sems.at[0, step], sems.at[1, owner], where)

    sources = (query_ref, key_ref, value_ref)
    map_copy = pltpu.make_async_copy(map_ref, map_held, local_sems.at[0])
    keep_copy = pltpu.make_async_copy(shard_ref, shard_rows(group), local_sems.at[1])
    embed_copy = pltpu.make_async_copy(embed_hbm, embed_ref, local_sems.at[2])
    weight_copy = pltpu.make_async_copy(weight_hbm, weight_ref, local_sems.at[3])

    greet([(peer, group) for peer in peers] + [(me, peer) for peer in peers_g])
    for episode in range(episodes):
        for tensor, source in enumerate(sources):
            for step, peer in enumerate(peers):
                swap_copy(tensor, source, episode, step, me, peer).start()
            my_copy(tensor, source, episode).start()
    for step, peer in reversed(list(enumerate(lines))):
        shard_copy(step, group, peer).start()
    pass_copy(n_out - 1, group, shard_ref).start()
    map_copy.start()
    keep_copy.start()
    embed_copy.start()
    weight_copy.start()

    scalar_copies = [
        pltpu.make_async_copy(source, target, scalar_sems.at[index])
        for index, (source, target) in enumerate(
            [
                (length_hbm, length_ref),
                (action_hbm, action_ref),
                (mask_hbm, mask_ref),
                (id_hbm, id_ref),
                (reward_hbm, reward_ref),
            ]
        )
    ]
    for copy in scalar_copies:
        copy.start()
    for copy in scalar_copies:
        copy.wait()

    lane = lax.broadcasted_iota(jnp.int32, (8, 128), 1)
    stats = jnp.zeros((8, 128), jnp.float32)
    for episode in range(episodes):
        reward, member = reward_ref[episode], id_ref[episode]
        stats = stats + jnp.where(lane == member, reward, 0.0)
        stats = stats + jnp.where(lane == group_count + member, reward * reward, 0.0)
        stats = stats + jnp.where(lane == 2 * group_count + member, 1.0, 0.0)
        for action in range(action_count):
            valid = mask_ref[episode, action].astype(jnp.float32)
            stats = stats + jnp.where(lane == 3 * group_count, valid, 0.0)
    stats_send[...] = stats
    stats_all[group] = stats
    for step, peer in enumerate(peers_g):
        to_all(stats_send, stats_all, stats_sems, step, group, (me, peer)).start()

    pooled_ref[...] = jnp.zeros_like(pooled_ref)
    head_rows[...] = jnp.zeros_like(head_rows)

    tall_query = min(seq, 256)

    def attend(episode):
        live = lax.broadcasted_iota(jnp.int32, (tall_query, seq), 1) < length_ref[episode]

        def one_head(head, carry):
            at = pl.ds(pl.multiple_of(head * HD, HD), HD)
            key_head = heads_all[1, episode, :, at]
            value_head = heads_all[2, episode, :, at]
            for first in range(0, seq, tall_query):
                query_head = heads_all[0, episode, first : first + tall_query, at]
                scores = lax.dot_general(
                    query_head, key_head, (((1,), (1,)), ((), ())), preferred_element_type=jnp.float32
                )
                scores = jnp.where(live, scores * (1.0 / math.sqrt(HD)), NEG_LARGE)
                probs = jnp.exp(scores - jnp.max(scores, axis=1, keepdims=True))
                row_total = jnp.sum(probs, axis=1, keepdims=True)
                weighted = jnp.dot(probs.astype(jnp.bfloat16), value_head, preferred_element_type=jnp.float32)
                blocks[me, episode * seq + first : episode * seq + first + tall_query, at] = (
                    weighted / row_total
                ).astype(jnp.bfloat16)
            return carry

        lax.fori_loop(0, width // HD, one_head, 0)

    tile = min(units, 512)
    per_band = units // tile
    bands = -(-features // (tile * per_band))
    staged = square and episodes == 2 and bands * seq <= features and seq % 128 == 0

    def add_frames(episode, first, tall, owners, opens, closes):
        for index, left in enumerate(range(0, features, tile)):
            lanes = min(tile, features - left)
            part = None
            for owner in owners:
                term = jnp.dot(
                    blocks[owner, episode * seq + first : episode * seq + first + tall, :],
                    map_held[pl.ds(pl.multiple_of(owner * width, 128), width), left : left + lanes],
                    preferred_element_type=jnp.float32,
                )
                part = term if part is None else part + term
            down, across = index // per_band * seq + first, index % per_band * tile
            held = (episode, slice(down, down + tall), slice(across, across + lanes))
            if not opens:
                part = part + moments[held]
            if closes:
                frames_ref[episode, first : first + tall, left : left + lanes] = part.astype(jnp.bfloat16)
            else:
                moments[held] = part

    def activate(episode, first, tall):
        length = jnp.full((tall, 1), length_ref[episode], jnp.int32)
        kept = lax.broadcasted_iota(jnp.int32, (tall, 1), 0) + first < length
        scale = jnp.where(kept, 1.0 / length.astype(jnp.float32), 0.0)
        for left in range(0, units, tile):
            at = slice(left, left + tile)
            pre_act = jnp.dot(
                frames_ref[episode, first : first + tall, :],
                columns_ref[:, at],
                preferred_element_type=jnp.float32,
            )
            below_it = 0.5 * (1.0 + lax.erf(pre_act * SQRT_HALF))
            pooled_ref[episode : episode + 1, at] += jnp.sum(
                scale * (pre_act * below_it), axis=0, keepdims=True
            )
            slope = below_it + pre_act * jnp.exp(-0.5 * pre_act * pre_act) * INV_ROOT_TAU
            slope_ref[episode, first : first + tall, at] = (scale * slope).astype(jnp.bfloat16)

    def find_moments(episode):
        for left in range(0, features, 256):
            at = slice(left, min(left + 256, features))
            moments[episode, at, :] = lax.dot_general(
                frames_ref[episode, :, at],
                slope_ref[episode],
                (((0,), (0,)), ((), ())),
                preferred_element_type=jnp.float32,
            )

    def wait_heads(episode):
        for tensor, source in enumerate(sources):
            my_copy(tensor, source, episode).wait()
            for peer in peers:
                swap_copy(tensor, source, episode, 0, peer, peer).wait_recv()

    def forward_shards():
        for step, peer in enumerate(lines):
            shard_copy(step, peer, peer).wait_recv()
            pass_copy(step, peer, columns_ref.at[pl.ds(pl.multiple_of(peer * chunk, 8), chunk), :]).start()

    def wait_columns():
        for step, peer in enumerate(lines):
            pass_copy(step, peer + 1 - 2 * core, shard_rows(peer)).wait_recv()
        pass_copy(n_out - 1, sibling, shard_ref).wait_recv()
        keep_copy.wait()

    def block_copy(strip, step, owner, peer, at, part):
        held = blocks.at[owner, pl.ds(*at), :]
        return remote(held, held, block_send.at[strip, step], block_recv.at[strip, owner, part], (peer, group))

    if staged:
        strips = [(0, first, seq // 2) for first in range(0, seq, seq // 2)]
        strips += [(1, first, seq // 4) for first in range(0, seq, seq // 4)]

        def whole_of(strip):
            episode, first, tall = strips[strip]
            return episode * seq + first, tall

        def half_of(strip, which):
            start, tall = whole_of(strip)
            return start + which * (tall // 2), tall // 2

        def own(strip):
            block_copy(strip, 0, me, row_peer, whole_of(strip), 0).start()
            block_copy(strip, 1, me, col_peer, whole_of(strip), 0).start()

        def forward(strip):
            block_copy(strip, 0, row_peer, row_peer, whole_of(strip), 0).wait_recv()
            block_copy(strip, 2, row_peer, col_peer, half_of(strip, 0), 0).start()
            block_copy(strip, 1, col_peer, col_peer, whole_of(strip), 0).wait_recv()
            block_copy(strip, 3, col_peer, row_peer, half_of(strip, 1), 1).start()

        def add_near(strip):
            add_frames(*strips[strip], [me, row_peer, col_peer], True, False)

        def add_far(strip):
            block_copy(strip, 2, far_peer, col_peer, half_of(strip, 0), 0).wait_recv()
            block_copy(strip, 3, far_peer, row_peer, half_of(strip, 1), 1).wait_recv()
            add_frames(*strips[strip], [far_peer], False, True)

        wait_heads(0)
        attend(0)
        own(0)
        own(1)
        wait_heads(1)
        attend(1)
        map_copy.wait()
        forward(0)
        add_near(0)
        forward(1)
        own(2)
        own(3)
        add_near(1)
        forward_shards()
        add_far(0)
        add_far(1)
        wait_columns()
        activate(*strips[0])
        forward(2)
        own(4)
        add_near(2)
        activate(*strips[1])
        forward(3)
        own(5)
        add_near(3)
        add_far(2)
        activate(*strips[2])
        find_moments(0)
        forward(4)
        add_near(4)
        add_far(3)
        activate(*strips[3])
        forward(5)
        add_near(5)
        add_far(4)
        activate(*strips[4])
        add_far(5)
        activate(*strips[5])
    else:
        tall = min(seq, 128)
        for episode in range(episodes):
            wait_heads(episode)
            attend(episode)
            for step, peer in enumerate(peers):
                block_copy(episode, step, me, peer, (episode * seq, seq), 0).start()
        map_copy.wait()
        forward_shards()
        wait_columns()
        for episode in range(episodes):
            for step, peer in enumerate(peers):
                block_copy(episode, step, peer, peer, (episode * seq, seq), 0).wait_recv()
            for first in range(0, seq, tall):
                add_frames(episode, first, tall, [me] + peers, True, True)
                activate(episode, first, tall)
            if episode < episodes - 1:
                find_moments(episode)

    embed_copy.wait()
    weight_copy.wait()
    for episode in range(episodes):
        head_rows[episode * action_count : (episode + 1) * action_count, :] = (
            pooled_ref[episode : episode + 1, :] + embed_ref[...]
        )
    head_ref[...] = head_rows[...].astype(jnp.bfloat16)
    partial = jnp.dot(head_ref[...], weight_ref[...], preferred_element_type=jnp.float32)
    logits_send[...] = partial
    logits_all[me] = partial
    for step, peer in enumerate(peers):
        to_all(logits_send, logits_all, logits_sems, step, me, (peer, group)).start()
    head_all[group] = head_ref[...]
    for step, peer in enumerate(peers_g):
        to_all(head_ref, head_all, head_sems, step, group, (me, peer)).start()

    find_moments(episodes - 1)

    for peer in peers_g:
        to_all(stats_send, stats_all, stats_sems, 0, peer, (me, peer)).wait_recv()
    stats = jnp.sum(stats_all[...], axis=0)[0:1]
    lane = lane[0:1]

    def entry(index):
        return jnp.sum(jnp.where(lane == index, stats, 0.0), axis=1, keepdims=True)

    mask_total = jnp.maximum(entry(3 * group_count), 1.0)
    row = lax.broadcasted_iota(jnp.int32, (rows, 1), 0)
    chosen = jnp.zeros((rows, 1), jnp.int32)
    loss_weight = jnp.zeros((rows, 1), jnp.float32)
    for episode in range(episodes):
        member = id_ref[episode]
        size = jnp.maximum(entry(2 * group_count + member), 1.0)
        mean = entry(member) / size
        variance = entry(group_count + member) / size - mean * mean
        advantage = (reward_ref[episode] - mean) / jnp.sqrt(jnp.maximum(variance, 1.0))
        for action in range(action_count):
            here = row == episode * action_count + action
            chosen = jnp.where(here, action_ref[episode, action], chosen)
            valid = mask_ref[episode, action].astype(jnp.float32)
            loss_weight = jnp.where(here, -valid * advantage / mask_total, loss_weight)
    picked = (lax.broadcasted_iota(jnp.int32, (rows, bins), 1) == chosen).astype(jnp.float32)

    for peer in peers:
        to_all(logits_send, logits_all, logits_sems, 0, peer, (peer, group)).wait_recv()
    logits = logits_all[0]
    for slot in range(1, n_cp):
        logits = logits + logits_all[slot]
    shifted = logits - jnp.max(logits, axis=1, keepdims=True)
    log_all = shifted - jnp.log(jnp.sum(jnp.exp(shifted), axis=1, keepdims=True))
    logprob = jnp.sum(picked * log_all, axis=1, keepdims=True)
    logit_grad = (loss_weight * (picked - jnp.exp(log_all))).astype(jnp.bfloat16)
    pull_back = lax.dot_general(
        logit_grad, weight_ref[...], (((1,), (1,)), ((), ())), preferred_element_type=jnp.float32
    )
    for episode in range(episodes):
        mine = jnp.logical_and(row >= episode * action_count, row < (episode + 1) * action_count)
        pulls[episode : episode + 1, :] = jnp.sum(jnp.where(mine, pull_back, 0.0), axis=0, keepdims=True)
    grad_send[...] = logit_grad
    grad_all[group] = logit_grad

    block = 16 if chunk % 16 == 0 else 8

    def fill(target, slot, part, terms):
        at = pl.ds(pl.multiple_of(part * span, 128), span)
        scales = [pulls[episode : episode + 1, at] for episode in range(episodes)]

        def some(index, carry):
            here = pl.ds(pl.multiple_of(index * block, block), block)
            down = pl.ds(pl.multiple_of(slot * chunk + index * block, 8), block)
            total = moments[0, down, at] * scales[0]
            for episode in range(1, episodes):
                total = total + moments[episode, down, at] * scales[episode]
            for term in terms:
                total = total + term[here, :].astype(jnp.float32)
            target[here, :] = total.astype(jnp.bfloat16)
            return carry

        lax.fori_loop(0, chunk // block, some, 0)

    def pair_copy(target, part):
        return remote(
            pair_send.at[target, part],
            pair_recv.at[target, part],
            pair_sems.at[0, target, part],
            pair_sems.at[1, target, part],
            (me, sibling),
        )

    def line_copy(slot, part, where):
        return remote(
            line_send.at[slot, part],
            line_recv.at[slot, part],
            line_sends.at[slot, part],
            line_recvs.at[slot, part],
            where,
        )

    def up_copy(target, part):
        return line_copy(target + 1, part, above)

    def down_copy(target, part):
        return line_copy(target, part, below)

    def give(target, part):
        fill(pair_send.at[target, part], 2 * target + 1 - core, part, [])
        pair_copy(target, part).start()

    def pass_on(target, part, slot, ends, copy):
        pair_copy(target, part).wait_recv()
        own_part = [pair_recv.at[target, part]]
        goal = line_send.at[slot, part]

        @pl.when(ends)
        def _():
            fill(goal, 2 * target + core, part, own_part)

        @pl.when(jnp.logical_not(ends))
        def _():
            copy(target, part).wait_recv()
            fill(goal, 2 * target + core, part, own_part + [line_recv.at[slot, part]])

        copy(target, part).start()

    steps = last * parts

    def give_at(index):
        time, part = lax.div(index, parts), lax.rem(index, parts)
        early = index < steps

        @pl.when(jnp.logical_and(early, time >= place))
        def _():
            give(last + place - time, part)

        @pl.when(jnp.logical_and(early, time >= last - place))
        def _():
            give(time - last + place, part)

        @pl.when(jnp.logical_not(early))
        def _():
            give(place, index - steps)

    def pass_at(index):
        time, part = lax.div(index, parts), lax.rem(index, parts)

        @pl.when(time >= place)
        def _():
            target = last + place - time
            pass_on(target, part, target + 1, place == 0, up_copy)

        @pl.when(time >= last - place)
        def _():
            target = time - last + place
            pass_on(target, part, target, place == last, down_copy)

    def open_up(index, carry):
        give_at(index)
        return carry

    def go_on(index, carry):
        give_at(index + parts)
        pass_at(index)

        @pl.when(index == 0)
        def _():
            for step, peer in enumerate(peers_g):
                to_all(grad_send, grad_all, grad_sems, step, group, (me, peer)).start()

        return carry

    lax.fori_loop(0, parts, open_up, 0)
    lax.fori_loop(0, steps, go_on, 0)

    cell = lax.broadcasted_iota(jnp.int32, (episodes, action_count), 0) * action_count
    cell = cell + lax.broadcasted_iota(jnp.int32, (episodes, action_count), 1)
    laid = jnp.zeros((episodes, action_count), jnp.float32)
    for index in range(episodes * action_count):
        laid = jnp.where(cell == index, logprob[index : index + 1, :], laid)
    logprob_ref[...] = laid
    logprob_out = pltpu.make_async_copy(logprob_ref, logprob_hbm, out_sems.at[0])
    logprob_out.start()
    for peer in peers_g:
        to_all(head_ref, head_all, head_sems, 0, peer, (me, peer)).wait_recv()
        to_all(grad_send, grad_all, grad_sems, 0, peer, (me, peer)).wait_recv()
    grad_head_ref[...] = lax.dot_general(
        head_all[...].reshape(n_grp * rows, units),
        grad_all[...].reshape(n_grp * rows, bins),
        (((0,), (0,)), ((), ())),
        preferred_element_type=jnp.float32,
    ).astype(jnp.bfloat16)
    grad_head_out = pltpu.make_async_copy(grad_head_ref, grad_head_hbm, out_sems.at[1])
    grad_head_out.start()

    def out_copy(part):
        at = pl.ds(part * span, span)
        return pltpu.make_async_copy(out_ref.at[:, at], out_hbm.at[:, at], out_sems.at[2 + part])

    for part in range(parts):
        goal = out_ref.at[:, pl.ds(part * span, span)]
        pair_copy(place, part).wait_recv()
        own_part = [pair_recv.at[place, part]]
        rose, fell = line_recv.at[place + 1, part], line_recv.at[place, part]

        @pl.when(place == 0)
        def _():
            down_copy(place, part).wait_recv()
            fill(goal, group, part, own_part + [fell])

        @pl.when(place == last)
        def _():
            up_copy(place, part).wait_recv()
            fill(goal, group, part, own_part + [rose])

        @pl.when(jnp.logical_and(place > 0, place < last))
        def _():
            up_copy(place, part).wait_recv()
            down_copy(place, part).wait_recv()
            fill(goal, group, part, own_part + [rose, fell])

        out_copy(part).start()

    for target in range(n_out):
        for part in range(parts):
            pair_copy(target, part).wait_send()

            @pl.when(target > place)
            def _():
                up_copy(target, part).wait_send()

            @pl.when(target < place)
            def _():
                down_copy(target, part).wait_send()

    for step, peer in enumerate(peers):
        to_all(logits_send, logits_all, logits_sems, step, me, (peer, group)).wait_send()
    for step, peer in enumerate(peers_g):
        to_all(stats_send, stats_all, stats_sems, step, group, (me, peer)).wait_send()
        to_all(head_ref, head_all, head_sems, step, group, (me, peer)).wait_send()
        to_all(grad_send, grad_all, grad_sems, step, group, (me, peer)).wait_send()
    for episode in range(episodes):
        for tensor, source in enumerate(sources):
            for step, peer in enumerate(peers):
                swap_copy(tensor, source, episode, step, me, peer).wait_send()
    if staged:
        for strip in range(len(strips)):
            block_copy(strip, 0, me, row_peer, whole_of(strip), 0).wait_send()
            block_copy(strip, 1, me, col_peer, whole_of(strip), 0).wait_send()
            block_copy(strip, 2, row_peer, col_peer, half_of(strip, 0), 0).wait_send()
            block_copy(strip, 3, col_peer, row_peer, half_of(strip, 1), 1).wait_send()
    else:
        for episode in range(episodes):
            for step, peer in enumerate(peers):
                block_copy(episode, step, me, peer, (episode * seq, seq), 0).wait_send()
    for step, peer in enumerate(lines):
        shard_copy(step, group, peer).wait_send()
        pass_copy(step, peer, shard_rows(peer)).wait_send()
    pass_copy(n_out - 1, group, shard_ref).wait_send()
    logprob_out.wait()
    grad_head_out.wait()
    for part in range(parts):
        out_copy(part).wait()


def train_step(
    queries,
    keys,
    values,
    lengths,
    frame_map,
    proj_weight,
    head_weight,
    act_embed,
    actions,
    action_mask,
    group_ids,
    rewards,
):
    n_cp, n_grp = lax.axis_size("cp"), lax.axis_size("grp")
    n_out = n_grp // 2
    episodes, tokens, att_width = queries.shape
    group_count = max(1, episodes * n_grp // 8)
    seq, width = tokens * n_cp, att_width // n_cp
    chunk, units = proj_weight.shape
    features = frame_map.shape[1]
    rows, bins = -(-actions.size // 16) * 16, head_weight.shape[1]
    parts = 2
    strips = episodes + 4
    anywhere = pl.BlockSpec(memory_space=pl.ANY)
    dma = pltpu.SemaphoreType.DMA
    bf16, f32 = jnp.bfloat16, jnp.float32
    return pl.pallas_call(
        lambda *refs: step_kernel(n_cp, n_out, group_count, parts, *refs),
        out_shape=(
            jax.ShapeDtypeStruct(actions.shape, f32),
            jax.ShapeDtypeStruct((chunk, units), bf16),
            jax.ShapeDtypeStruct((units, bins), bf16),
        ),
        in_specs=[anywhere] * 12,
        out_specs=(anywhere,) * 3,
        scratch_shapes=[
            pltpu.SMEM(lengths.shape, lengths.dtype),
            pltpu.SMEM(actions.shape, actions.dtype),
            pltpu.SMEM(action_mask.shape, action_mask.dtype),
            pltpu.SMEM(group_ids.shape, group_ids.dtype),
            pltpu.SMEM(rewards.shape, f32),
            pltpu.VMEM(actions.shape, f32),
            pltpu.VMEM((chunk, units), bf16),
            pltpu.VMEM((units, bins), bf16),
            pltpu.VMEM((3, episodes, seq, width), bf16),
            pltpu.VMEM((n_cp, episodes * seq, width), bf16),
            pltpu.VMEM(frame_map.shape, bf16),
            pltpu.VMEM((n_grp * chunk, units), bf16),
            pltpu.VMEM((episodes, seq, features), bf16),
            pltpu.VMEM((episodes, seq, units), bf16),
            pltpu.VMEM((episodes, features, units), f32),
            pltpu.VMEM((-(-episodes // 8) * 8, units), f32),
            pltpu.VMEM(act_embed.shape, f32),
            pltpu.VMEM(head_weight.shape, bf16),
            pltpu.VMEM((rows, units), f32),
            pltpu.VMEM((rows, units), bf16),
            pltpu.VMEM((rows, bins), f32),
            pltpu.VMEM((n_cp, rows, bins), f32),
            pltpu.VMEM((8, 128), f32),
            pltpu.VMEM((n_grp, 8, 128), f32),
            pltpu.VMEM((n_grp, rows, units), bf16),
            pltpu.VMEM((rows, bins), bf16),
            pltpu.VMEM((n_grp, rows, bins), bf16),
            pltpu.VMEM((-(-episodes // 8) * 8, units), f32),
            pltpu.VMEM((n_out, parts, chunk, units // parts), bf16),
            pltpu.VMEM((n_out, parts, chunk, units // parts), bf16),
            pltpu.VMEM((n_out + 1, parts, chunk, units // parts), bf16),
            pltpu.VMEM((n_out + 1, parts, chunk, units // parts), bf16),
            dma((4 + 3 * episodes,)),
            dma((3, episodes, n_cp)),
            dma((3, episodes, n_cp)),
            dma((strips, max(n_cp, 4))),
            dma((strips, n_cp, 2)),
            dma((n_out,)),
            dma((n_grp,)),
            dma((n_out,)),
            dma((n_grp,)),
            dma((2, n_cp)),
            dma((2, n_grp)),
            dma((2, n_grp)),
            dma((2, n_grp)),
            dma((2, n_out, parts)),
            dma((n_out + 1, parts)),
            dma((n_out + 1, parts)),
            dma((5,)),
            dma((2 + parts,)),
        ],
        compiler_params=pltpu.CompilerParams(
            collective_id=1, has_side_effects=True, vmem_limit_bytes=62 * 1024 * 1024
        ),
        name="train_step",
    )(
        lengths,
        actions,
        action_mask,
        group_ids,
        rewards,
        queries,
        keys,
        values,
        frame_map,
        proj_weight,
        act_embed,
        head_weight,
    )


def write_kernel(first, second, third, first_out, second_out, third_out):
    first_out[...] = first[...]
    second_out[...] = second[...]
    third_out[...] = third[...]


def write_out(*results):
    in_vmem = pl.BlockSpec(memory_space=pltpu.VMEM)
    return pl.pallas_call(
        write_kernel,
        out_shape=tuple(jax.ShapeDtypeStruct(result.shape, result.dtype) for result in results),
        in_specs=[in_vmem] * 3,
        out_specs=(in_vmem,) * 3,
        name="write_out",
    )(*results)


def per_device(*arrays):
    return write_out(*train_step(*arrays))


def solution(mesh):
    in_specs = (
        P("grp", "cp", None),
        P("grp", "cp", None),
        P("grp", "cp", None),
        P("grp"),
        P(),
        P("grp", "cp"),
        P("cp", None),
        P(None, "cp"),
        P("grp", None),
        P("grp", None),
        P("grp"),
        P("grp"),
    )
    out_specs = (P("grp", None), P("grp", "cp"), P("cp", None))
    return jax.shard_map(
        per_device, mesh=mesh, in_specs=in_specs, out_specs=out_specs, check_vma=False
    )
```

```python
import math

import jax
import jax.numpy as jnp
from jax import lax
from jax.experimental import pallas as pl
from jax.experimental.pallas import tpu as pltpu
from jax.sharding import PartitionSpec as P

HD = 128
ON_MESH = pl.DeviceIdType.MESH

SQRT_HALF = 0.7071067811865476
INV_ROOT_TAU = 0.3989422804014327
NEG_LARGE = -1e30


def remote(source, target, send_sem, recv_sem, where):
    return pltpu.make_async_remote_copy(
        src_ref=source,
        dst_ref=target,
        send_sem=send_sem,
        recv_sem=recv_sem,
        device_id=where,
        device_id_type=ON_MESH,
    )


def greet(peers):
    barrier = pltpu.get_barrier_semaphore()
    for where in peers:
        pl.semaphore_signal(barrier, inc=1, device_id=where, device_id_type=ON_MESH)
    pl.semaphore_wait(barrier, len(peers))


def step_kernel(
    n_cp,
    n_out,
    group_count,
    parts,
    length_hbm,
    action_hbm,
    mask_hbm,
    id_hbm,
    reward_hbm,
    query_ref,
    key_ref,
    value_ref,
    map_ref,
    shard_ref,
    embed_hbm,
    weight_hbm,
    logprob_hbm,
    out_hbm,
    grad_head_hbm,
    length_ref,
    action_ref,
    mask_ref,
    id_ref,
    reward_ref,
    logprob_ref,
    out_ref,
    grad_head_ref,
    heads_all,
    blocks,
    map_held,
    columns_ref,
    frames_ref,
    slope_ref,
    moments,
    pooled_ref,
    embed_ref,
    weight_ref,
    head_rows,
    head_ref,
    logits_send,
    logits_all,
    stats_send,
    stats_all,
    head_all,
    grad_send,
    grad_all,
    pulls,
    pair_send,
    pair_recv,
    line_send,
    line_recv,
    local_sems,
    swap_send,
    swap_recv,
    block_send,
    block_recv,
    shard_send,
    shard_recv,
    pass_send,
    pass_recv,
    logits_sems,
    stats_sems,
    head_sems,
    grad_sems,
    pair_sems,
    line_sends,
    line_recvs,
    scalar_sems,
    out_sems,
):
    episodes, tokens, _ = query_ref.shape
    action_count = action_ref.shape[1]
    width = blocks.shape[2]
    seq = tokens * n_cp
    features, units = columns_ref.shape
    chunk = shard_ref.shape[0]
    rows, bins = logits_send.shape
    span = pair_send.shape[3]
    n_grp = 2 * n_out
    last = n_out - 1
    me, group = lax.axis_index("cp"), lax.axis_index("grp")
    place, core = group // 2, lax.rem(group, 2)
    sibling = 2 * place + 1 - core
    above, below = (me, lax.rem(group + 2, n_grp)), (me, lax.rem(group + n_grp - 2, n_grp))
    square = n_cp == 4
    if square:
        row_peer = me + 1 - 2 * lax.rem(me, 2)
        col_peer = lax.rem(me + 2, 4)
        far_peer = lax.rem(row_peer + 2, 4)
        peers = [far_peer, row_peer, col_peer]
    else:
        peers = [lax.rem(me + step, n_cp) for step in range(1, n_cp)]
    lines = [2 * lax.rem(place + step, n_out) + core for step in range(1, n_out)]
    peers_g = [lax.rem(group + step, n_grp) for step in range(1, n_grp)]

    def shard_rows(owner):
        return columns_ref.at[pl.ds(pl.multiple_of(owner * chunk, 8), chunk), :]

    def my_copy(tensor, source, episode):
        return pltpu.make_async_copy(
            source.at[episode, :, pl.ds(pl.multiple_of(me * width, 128), width)],
            heads_all.at[tensor, episode, pl.ds(pl.multiple_of(me * tokens, 8), tokens), :],
            local_sems.at[4 + tensor * episodes + episode],
        )

    def swap_copy(tensor, source, episode, step, owner, peer):
        return remote(
            source.at[episode, :, pl.ds(pl.multiple_of(peer * width, 128), width)],
            heads_all.at[tensor, episode, pl.ds(pl.multiple_of(owner * tokens, 8), tokens), :],
            swap_send.at[tensor, episode, step],
            swap_recv.at[tensor, episode, owner],
            (peer, group),
        )

    def shard_copy(step, owner, peer):
        return remote(shard_ref, shard_rows(owner), shard_send.at[step], shard_recv.at[owner], (me, peer))

    def pass_copy(step, owner, source):
        return remote(source, shard_rows(owner), pass_send.at[step], pass_recv.at[owner], (me, sibling))

    def to_all(send, everyone, sems, step, owner, where):
        return remote(send, everyone.at[owner], sems.at[0, step], sems.at[1, owner], where)

    sources = (query_ref, key_ref, value_ref)
    map_copy = pltpu.make_async_copy(map_ref, map_held, local_sems.at[0])
    keep_copy = pltpu.make_async_copy(shard_ref, shard_rows(group), local_sems.at[1])
    embed_copy = pltpu.make_async_copy(embed_hbm, embed_ref, local_sems.at[2])
    weight_copy = pltpu.make_async_copy(weight_hbm, weight_ref, local_sems.at[3])

    greet([(peer, group) for peer in peers] + [(me, peer) for peer in peers_g])
    for episode in range(episodes):
        for tensor, source in enumerate(sources):
            for step, peer in enumerate(peers):
                swap_copy(tensor, source, episode, step, me, peer).start()
            my_copy(tensor, source, episode).start()
    for step, peer in reversed(list(enumerate(lines))):
        shard_copy(step, group, peer).start()
    pass_copy(n_out - 1, group, shard_ref).start()
    map_copy.start()
    keep_copy.start()
    embed_copy.start()
    weight_copy.start()

    scalar_copies = [
        pltpu.make_async_copy(source, target, scalar_sems.at[index])
        for index, (source, target) in enumerate(
            [
                (length_hbm, length_ref),
                (action_hbm, action_ref),
                (mask_hbm, mask_ref),
                (id_hbm, id_ref),
                (reward_hbm, reward_ref),
            ]
        )
    ]
    for copy in scalar_copies:
        copy.start()
    for copy in scalar_copies:
        copy.wait()

    lane = lax.broadcasted_iota(jnp.int32, (8, 128), 1)
    stats = jnp.zeros((8, 128), jnp.float32)
    for episode in range(episodes):
        reward, member = reward_ref[episode], id_ref[episode]
        stats = stats + jnp.where(lane == member, reward, 0.0)
        stats = stats + jnp.where(lane == group_count + member, reward * reward, 0.0)
        stats = stats + jnp.where(lane == 2 * group_count + member, 1.0, 0.0)
        for action in range(action_count):
            valid = mask_ref[episode, action].astype(jnp.float32)
            stats = stats + jnp.where(lane == 3 * group_count, valid, 0.0)
    stats_send[...] = stats
    stats_all[group] = stats
    for step, peer in enumerate(peers_g):
        to_all(stats_send, stats_all, stats_sems, step, group, (me, peer)).start()

    pooled_ref[...] = jnp.zeros_like(pooled_ref)
    head_rows[...] = jnp.zeros_like(head_rows)

    tall_query = min(seq, 256)

    def attend(episode):
        live = lax.broadcasted_iota(jnp.int32, (tall_query, seq), 1) < length_ref[episode]

        def one_head(head, carry):
            at = pl.ds(pl.multiple_of(head * HD, HD), HD)
            key_head = heads_all[1, episode, :, at]
            value_head = heads_all[2, episode, :, at]
            for first in range(0, seq, tall_query):
                query_head = heads_all[0, episode, first : first + tall_query, at]
                scores = lax.dot_general(
                    query_head, key_head, (((1,), (1,)), ((), ())), preferred_element_type=jnp.float32
                )
                scores = jnp.where(live, scores * (1.0 / math.sqrt(HD)), NEG_LARGE)
                probs = jnp.exp(scores - jnp.max(scores, axis=1, keepdims=True))
                row_total = jnp.sum(probs, axis=1, keepdims=True)
                weighted = jnp.dot(probs.astype(jnp.bfloat16), value_head, preferred_element_type=jnp.float32)
                blocks[me, episode * seq + first : episode * seq + first + tall_query, at] = (
                    weighted / row_total
                ).astype(jnp.bfloat16)
            return carry

        lax.fori_loop(0, width // HD, one_head, 0)

    tile = min(units, 512)
    per_band = units // tile
    bands = -(-features // (tile * per_band))
    staged = square and episodes == 2 and bands * seq <= features and seq % 128 == 0

    def add_frames(episode, first, tall, owners, opens, closes):
        for index, left in enumerate(range(0, features, tile)):
            lanes = min(tile, features - left)
            part = None
            for owner in owners:
                term = jnp.dot(
                    blocks[owner, episode * seq + first : episode * seq + first + tall, :],
                    map_held[pl.ds(pl.multiple_of(owner * width, 128), width), left : left + lanes],
                    preferred_element_type=jnp.float32,
                )
                part = term if part is None else part + term
            down, across = index // per_band * seq + first, index % per_band * tile
            held = (episode, slice(down, down + tall), slice(across, across + lanes))
            if not opens:
                part = part + moments[held]
            if closes:
                frames_ref[episode, first : first + tall, left : left + lanes] = part.astype(jnp.bfloat16)
            else:
                moments[held] = part

    def activate(episode, first, tall):
        length = jnp.full((tall, 1), length_ref[episode], jnp.int32)
        kept = lax.broadcasted_iota(jnp.int32, (tall, 1), 0) + first < length
        scale = jnp.where(kept, 1.0 / length.astype(jnp.float32), 0.0)
        for left in range(0, units, tile):
            at = slice(left, left + tile)
            pre_act = jnp.dot(
                frames_ref[episode, first : first + tall, :],
                columns_ref[:, at],
                preferred_element_type=jnp.float32,
            )
            below_it = 0.5 * (1.0 + lax.erf(pre_act * SQRT_HALF))
            pooled_ref[episode : episode + 1, at] += jnp.sum(
                scale * (pre_act * below_it), axis=0, keepdims=True
            )
            slope = below_it + pre_act * jnp.exp(-0.5 * pre_act * pre_act) * INV_ROOT_TAU
            slope_ref[episode, first : first + tall, at] = (scale * slope).astype(jnp.bfloat16)

    def find_moments(episode):
        for left in range(0, features, 256):
            at = slice(left, min(left + 256, features))
            moments[episode, at, :] = lax.dot_general(
                frames_ref[episode, :, at],
                slope_ref[episode],
                (((0,), (0,)), ((), ())),
                preferred_element_type=jnp.float32,
            )

    def wait_heads(episode):
        for tensor, source in enumerate(sources):
            my_copy(tensor, source, episode).wait()
            for peer in peers:
                swap_copy(tensor, source, episode, 0, peer, peer).wait_recv()

    def forward_shards():
        for step, peer in enumerate(lines):
            shard_copy(step, peer, peer).wait_recv()
            pass_copy(step, peer, columns_ref.at[pl.ds(pl.multiple_of(peer * chunk, 8), chunk), :]).start()

    def wait_columns():
        for step, peer in enumerate(lines):
            pass_copy(step, peer + 1 - 2 * core, shard_rows(peer)).wait_recv()
        pass_copy(n_out - 1, sibling, shard_ref).wait_recv()
        keep_copy.wait()

    def block_copy(strip, step, owner, peer, at, part):
        held = blocks.at[owner, pl.ds(*at), :]
        return remote(held, held, block_send.at[strip, step], block_recv.at[strip, owner, part], (peer, group))

    if staged:
        strips = [(0, first, seq // 2) for first in range(0, seq, seq // 2)]
        strips += [(1, first, seq // 4) for first in range(0, seq, seq // 4)]

        def whole_of(strip):
            episode, first, tall = strips[strip]
            return episode * seq + first, tall

        def half_of(strip, which):
            start, tall = whole_of(strip)
            return start + which * (tall // 2), tall // 2

        def own(strip):
            block_copy(strip, 0, me, row_peer, whole_of(strip), 0).start()
            block_copy(strip, 1, me, col_peer, whole_of(strip), 0).start()

        def forward(strip):
            block_copy(strip, 0, row_peer, row_peer, whole_of(strip), 0).wait_recv()
            block_copy(strip, 2, row_peer, col_peer, half_of(strip, 0), 0).start()
            block_copy(strip, 1, col_peer, col_peer, whole_of(strip), 0).wait_recv()
            block_copy(strip, 3, col_peer, row_peer, half_of(strip, 1), 1).start()

        def add_near(strip):
            add_frames(*strips[strip], [me, row_peer, col_peer], True, False)

        def add_far(strip):
            block_copy(strip, 2, far_peer, col_peer, half_of(strip, 0), 0).wait_recv()
            block_copy(strip, 3, far_peer, row_peer, half_of(strip, 1), 1).wait_recv()
            add_frames(*strips[strip], [far_peer], False, True)

        wait_heads(0)
        attend(0)
        own(0)
        own(1)
        wait_heads(1)
        attend(1)
        map_copy.wait()
        forward(0)
        add_near(0)
        forward(1)
        own(2)
        own(3)
        add_near(1)
        forward_shards()
        add_far(0)
        add_far(1)
        wait_columns()
        activate(*strips[0])
        forward(2)
        own(4)
        add_near(2)
        activate(*strips[1])
        forward(3)
        own(5)
        add_near(3)
        add_far(2)
        activate(*strips[2])
        find_moments(0)
        forward(4)
        add_near(4)
        add_far(3)
        activate(*strips[3])
        forward(5)
        add_near(5)
        add_far(4)
        activate(*strips[4])
        add_far(5)
        activate(*strips[5])
    else:
        tall = min(seq, 128)
        for episode in range(episodes):
            wait_heads(episode)
            attend(episode)
            for step, peer in enumerate(peers):
                block_copy(episode, step, me, peer, (episode * seq, seq), 0).start()
        map_copy.wait()
        forward_shards()
        wait_columns()
        for episode in range(episodes):
            for step, peer in enumerate(peers):
                block_copy(episode, step, peer, peer, (episode * seq, seq), 0).wait_recv()
            for first in range(0, seq, tall):
                add_frames(episode, first, tall, [me] + peers, True, True)
                activate(episode, first, tall)
            if episode < episodes - 1:
                find_moments(episode)

    embed_copy.wait()
    weight_copy.wait()
    for episode in range(episodes):
        head_rows[episode * action_count : (episode + 1) * action_count, :] = (
            pooled_ref[episode : episode + 1, :] + embed_ref[...]
        )
    head_ref[...] = head_rows[...].astype(jnp.bfloat16)
    partial = jnp.dot(head_ref[...], weight_ref[...], preferred_element_type=jnp.float32)
    logits_send[...] = partial
    logits_all[me] = partial
    for step, peer in enumerate(peers):
        to_all(logits_send, logits_all, logits_sems, step, me, (peer, group)).start()
    head_all[group] = head_ref[...]
    for step, peer in enumerate(peers_g):
        to_all(head_ref, head_all, head_sems, step, group, (me, peer)).start()

    find_moments(episodes - 1)

    for peer in peers_g:
        to_all(stats_send, stats_all, stats_sems, 0, peer, (me, peer)).wait_recv()
    stats = jnp.sum(stats_all[...], axis=0)[0:1]
    lane = lane[0:1]

    def entry(index):
        return jnp.sum(jnp.where(lane == index, stats, 0.0), axis=1, keepdims=True)

    mask_total = jnp.maximum(entry(3 * group_count), 1.0)
    row = lax.broadcasted_iota(jnp.int32, (rows, 1), 0)
    chosen = jnp.zeros((rows, 1), jnp.int32)
    loss_weight = jnp.zeros((rows, 1), jnp.float32)
    for episode in range(episodes):
        member = id_ref[episode]
        size = jnp.maximum(entry(2 * group_count + member), 1.0)
        mean = entry(member) / size
        variance = entry(group_count + member) / size - mean * mean
        advantage = (reward_ref[episode] - mean) / jnp.sqrt(jnp.maximum(variance, 1.0))
        for action in range(action_count):
            here = row == episode * action_count + action
            chosen = jnp.where(here, action_ref[episode, action], chosen)
            valid = mask_ref[episode, action].astype(jnp.float32)
            loss_weight = jnp.where(here, -valid * advantage / mask_total, loss_weight)
    picked = (lax.broadcasted_iota(jnp.int32, (rows, bins), 1) == chosen).astype(jnp.float32)

    for peer in peers:
        to_all(logits_send, logits_all, logits_sems, 0, peer, (peer, group)).wait_recv()
    logits = logits_all[0]
    for slot in range(1, n_cp):
        logits = logits + logits_all[slot]
    shifted = logits - jnp.max(logits, axis=1, keepdims=True)
    log_all = shifted - jnp.log(jnp.sum(jnp.exp(shifted), axis=1, keepdims=True))
    logprob = jnp.sum(picked * log_all, axis=1, keepdims=True)
    logit_grad = (loss_weight * (picked - jnp.exp(log_all))).astype(jnp.bfloat16)
    grad_send[...] = logit_grad
    mates = lines + [sibling]
    for step, peer in enumerate(mates):
        to_all(grad_send, grad_all, grad_sems, step, group, (me, peer)).start()
    pull_back = lax.dot_general(
        logit_grad, weight_ref[...], (((1,), (1,)), ((), ())), preferred_element_type=jnp.float32
    )
    for episode in range(episodes):
        mine = jnp.logical_and(row >= episode * action_count, row < (episode + 1) * action_count)
        pulls[episode : episode + 1, :] = jnp.sum(jnp.where(mine, pull_back, 0.0), axis=0, keepdims=True)

    block = 16 if chunk % 16 == 0 else 8

    def fill(target, slot, part, terms):
        at = pl.ds(pl.multiple_of(part * span, 128), span)
        scales = [pulls[episode : episode + 1, at] for episode in range(episodes)]

        def some(index, carry):
            here = pl.ds(pl.multiple_of(index * block, block), block)
            down = pl.ds(pl.multiple_of(slot * chunk + index * block, 8), block)
            total = moments[0, down, at] * scales[0]
            for episode in range(1, episodes):
                total = total + moments[episode, down, at] * scales[episode]
            for term in terms:
                total = total + term[here, :].astype(jnp.float32)
            target[here, :] = total.astype(jnp.bfloat16)
            return carry

        lax.fori_loop(0, chunk // block, some, 0)

    def pair_copy(target, part):
        return remote(
            pair_send.at[target, part],
            pair_recv.at[target, part],
            pair_sems.at[0, target, part],
            pair_sems.at[1, target, part],
            (me, sibling),
        )

    def line_copy(slot, part, where):
        return remote(
            line_send.at[slot, part],
            line_recv.at[slot, part],
            line_sends.at[slot, part],
            line_recvs.at[slot, part],
            where,
        )

    def up_copy(target, part):
        return line_copy(target + 1, part, above)

    def down_copy(target, part):
        return line_copy(target, part, below)

    def give(target, part):
        fill(pair_send.at[target, part], 2 * target + 1 - core, part, [])
        pair_copy(target, part).start()

    def pass_on(target, part, slot, ends, copy):
        pair_copy(target, part).wait_recv()
        own_part = [pair_recv.at[target, part]]
        goal = line_send.at[slot, part]

        @pl.when(ends)
        def _():
            fill(goal, 2 * target + core, part, own_part)

        @pl.when(jnp.logical_not(ends))
        def _():
            copy(target, part).wait_recv()
            fill(goal, 2 * target + core, part, own_part + [line_recv.at[slot, part]])

        copy(target, part).start()

    steps = last * parts

    def give_at(index):
        time, part = lax.div(index, parts), lax.rem(index, parts)
        early = index < steps

        @pl.when(jnp.logical_and(early, time >= place))
        def _():
            give(last + place - time, part)

        @pl.when(jnp.logical_and(early, time >= last - place))
        def _():
            give(time - last + place, part)

        @pl.when(jnp.logical_not(early))
        def _():
            give(place, index - steps)

    def pass_at(index):
        time, part = lax.div(index, parts), lax.rem(index, parts)

        @pl.when(time >= place)
        def _():
            target = last + place - time
            pass_on(target, part, target + 1, place == 0, up_copy)

        @pl.when(time >= last - place)
        def _():
            target = time - last + place
            pass_on(target, part, target, place == last, down_copy)

    def open_up(index, carry):
        give_at(index)
        return carry

    def go_on(index, carry):
        give_at(index + parts)
        pass_at(index)
        return carry

    lax.fori_loop(0, parts, open_up, 0)
    lax.fori_loop(0, steps, go_on, 0)

    grad_all[group] = logit_grad
    for step, peer in enumerate(lines):
        to_all(grad_send, grad_all, grad_sems, 0, peer, (me, peer)).wait_recv()
        to_all(grad_all.at[peer], grad_all, grad_sems, n_out + step, peer, (me, sibling)).start()

    cell = lax.broadcasted_iota(jnp.int32, (episodes, action_count), 0) * action_count
    cell = cell + lax.broadcasted_iota(jnp.int32, (episodes, action_count), 1)
    laid = jnp.zeros((episodes, action_count), jnp.float32)
    for index in range(episodes * action_count):
        laid = jnp.where(cell == index, logprob[index : index + 1, :], laid)
    logprob_ref[...] = laid
    logprob_out = pltpu.make_async_copy(logprob_ref, logprob_hbm, out_sems.at[0])
    logprob_out.start()
    for peer in peers_g:
        to_all(head_ref, head_all, head_sems, 0, peer, (me, peer)).wait_recv()
    to_all(grad_send, grad_all, grad_sems, 0, sibling, (me, sibling)).wait_recv()
    for step, peer in enumerate(lines):
        other = peer + 1 - 2 * core
        to_all(grad_send, grad_all, grad_sems, 0, other, (me, sibling)).wait_recv()
    grad_head_ref[...] = lax.dot_general(
        head_all[...].reshape(n_grp * rows, units),
        grad_all[...].reshape(n_grp * rows, bins),
        (((0,), (0,)), ((), ())),
        preferred_element_type=jnp.float32,
    ).astype(jnp.bfloat16)
    grad_head_out = pltpu.make_async_copy(grad_head_ref, grad_head_hbm, out_sems.at[1])
    grad_head_out.start()

    def out_copy(part):
        at = pl.ds(part * span, span)
        return pltpu.make_async_copy(out_ref.at[:, at], out_hbm.at[:, at], out_sems.at[2 + part])

    for part in range(parts):
        goal = out_ref.at[:, pl.ds(part * span, span)]
        pair_copy(place, part).wait_recv()
        own_part = [pair_recv.at[place, part]]
        rose, fell = line_recv.at[place + 1, part], line_recv.at[place, part]

        @pl.when(place == 0)
        def _():
            down_copy(place, part).wait_recv()
            fill(goal, group, part, own_part + [fell])

        @pl.when(place == last)
        def _():
            up_copy(place, part).wait_recv()
            fill(goal, group, part, own_part + [rose])

        @pl.when(jnp.logical_and(place > 0, place < last))
        def _():
            up_copy(place, part).wait_recv()
            down_copy(place, part).wait_recv()
            fill(goal, group, part, own_part + [rose, fell])

        out_copy(part).start()

    for target in range(n_out):
        for part in range(parts):
            pair_copy(target, part).wait_send()

            @pl.when(target > place)
            def _():
                up_copy(target, part).wait_send()

            @pl.when(target < place)
            def _():
                down_copy(target, part).wait_send()

    for step, peer in enumerate(peers):
        to_all(logits_send, logits_all, logits_sems, step, me, (peer, group)).wait_send()
    for step, peer in enumerate(peers_g):
        to_all(stats_send, stats_all, stats_sems, step, group, (me, peer)).wait_send()
        to_all(head_ref, head_all, head_sems, step, group, (me, peer)).wait_send()
    for step, peer in enumerate(mates):
        to_all(grad_send, grad_all, grad_sems, step, group, (me, peer)).wait_send()
    for step, peer in enumerate(lines):
        to_all(grad_all.at[peer], grad_all, grad_sems, n_out + step, peer, (me, sibling)).wait_send()
    for episode in range(episodes):
        for tensor, source in enumerate(sources):
            for step, peer in enumerate(peers):
                swap_copy(tensor, source, episode, step, me, peer).wait_send()
    if staged:
        for strip in range(len(strips)):
            block_copy(strip, 0, me, row_peer, whole_of(strip), 0).wait_send()
            block_copy(strip, 1, me, col_peer, whole_of(strip), 0).wait_send()
            block_copy(strip, 2, row_peer, col_peer, half_of(strip, 0), 0).wait_send()
            block_copy(strip, 3, col_peer, row_peer, half_of(strip, 1), 1).wait_send()
    else:
        for episode in range(episodes):
            for step, peer in enumerate(peers):
                block_copy(episode, step, me, peer, (episode * seq, seq), 0).wait_send()
    for step, peer in enumerate(lines):
        shard_copy(step, group, peer).wait_send()
        pass_copy(step, peer, shard_rows(peer)).wait_send()
    pass_copy(n_out - 1, group, shard_ref).wait_send()
    logprob_out.wait()
    grad_head_out.wait()
    for part in range(parts):
        out_copy(part).wait()


def train_step(
    queries,
    keys,
    values,
    lengths,
    frame_map,
    proj_weight,
    head_weight,
    act_embed,
    actions,
    action_mask,
    group_ids,
    rewards,
):
    n_cp, n_grp = lax.axis_size("cp"), lax.axis_size("grp")
    n_out = n_grp // 2
    episodes, tokens, att_width = queries.shape
    group_count = max(1, episodes * n_grp // 8)
    seq, width = tokens * n_cp, att_width // n_cp
    chunk, units = proj_weight.shape
    features = frame_map.shape[1]
    rows, bins = -(-actions.size // 16) * 16, head_weight.shape[1]
    parts = 2
    strips = episodes + 4
    anywhere = pl.BlockSpec(memory_space=pl.ANY)
    dma = pltpu.SemaphoreType.DMA
    bf16, f32 = jnp.bfloat16, jnp.float32
    return pl.pallas_call(
        lambda *refs: step_kernel(n_cp, n_out, group_count, parts, *refs),
        out_shape=(
            jax.ShapeDtypeStruct(actions.shape, f32),
            jax.ShapeDtypeStruct((chunk, units), bf16),
            jax.ShapeDtypeStruct((units, bins), bf16),
        ),
        in_specs=[anywhere] * 12,
        out_specs=(anywhere,) * 3,
        scratch_shapes=[
            pltpu.SMEM(lengths.shape, lengths.dtype),
            pltpu.SMEM(actions.shape, actions.dtype),
            pltpu.SMEM(action_mask.shape, action_mask.dtype),
            pltpu.SMEM(group_ids.shape, group_ids.dtype),
            pltpu.SMEM(rewards.shape, f32),
            pltpu.VMEM(actions.shape, f32),
            pltpu.VMEM((chunk, units), bf16),
            pltpu.VMEM((units, bins), bf16),
            pltpu.VMEM((3, episodes, seq, width), bf16),
            pltpu.VMEM((n_cp, episodes * seq, width), bf16),
            pltpu.VMEM(frame_map.shape, bf16),
            pltpu.VMEM((n_grp * chunk, units), bf16),
            pltpu.VMEM((episodes, seq, features), bf16),
            pltpu.VMEM((episodes, seq, units), bf16),
            pltpu.VMEM((episodes, features, units), f32),
            pltpu.VMEM((-(-episodes // 8) * 8, units), f32),
            pltpu.VMEM(act_embed.shape, f32),
            pltpu.VMEM(head_weight.shape, bf16),
            pltpu.VMEM((rows, units), f32),
            pltpu.VMEM((rows, units), bf16),
            pltpu.VMEM((rows, bins), f32),
            pltpu.VMEM((n_cp, rows, bins), f32),
            pltpu.VMEM((8, 128), f32),
            pltpu.VMEM((n_grp, 8, 128), f32),
            pltpu.VMEM((n_grp, rows, units), bf16),
            pltpu.VMEM((rows, bins), bf16),
            pltpu.VMEM((n_grp, rows, bins), bf16),
            pltpu.VMEM((-(-episodes // 8) * 8, units), f32),
            pltpu.VMEM((n_out, parts, chunk, units // parts), bf16),
            pltpu.VMEM((n_out, parts, chunk, units // parts), bf16),
            pltpu.VMEM((n_out + 1, parts, chunk, units // parts), bf16),
            pltpu.VMEM((n_out + 1, parts, chunk, units // parts), bf16),
            dma((4 + 3 * episodes,)),
            dma((3, episodes, n_cp)),
            dma((3, episodes, n_cp)),
            dma((strips, max(n_cp, 4))),
            dma((strips, n_cp, 2)),
            dma((n_out,)),
            dma((n_grp,)),
            dma((n_out,)),
            dma((n_grp,)),
            dma((2, n_cp)),
            dma((2, n_grp)),
            dma((2, n_grp)),
            dma((2, n_grp)),
            dma((2, n_out, parts)),
            dma((n_out + 1, parts)),
            dma((n_out + 1, parts)),
            dma((5,)),
            dma((2 + parts,)),
        ],
        compiler_params=pltpu.CompilerParams(
            collective_id=1, has_side_effects=True, vmem_limit_bytes=62 * 1024 * 1024
        ),
        name="train_step",
    )(
        lengths,
        actions,
        action_mask,
        group_ids,
        rewards,
        queries,
        keys,
        values,
        frame_map,
        proj_weight,
        act_embed,
        head_weight,
    )


def write_kernel(first, second, third, first_out, second_out, third_out):
    first_out[...] = first[...]
    second_out[...] = second[...]
    third_out[...] = third[...]


def write_out(*results):
    in_vmem = pl.BlockSpec(memory_space=pltpu.VMEM)
    return pl.pallas_call(
        write_kernel,
        out_shape=tuple(jax.ShapeDtypeStruct(result.shape, result.dtype) for result in results),
        in_specs=[in_vmem] * 3,
        out_specs=(in_vmem,) * 3,
        name="write_out",
    )(*results)


def per_device(*arrays):
    return write_out(*train_step(*arrays))


def solution(mesh):
    in_specs = (
        P("grp", "cp", None),
        P("grp", "cp", None),
        P("grp", "cp", None),
        P("grp"),
        P(),
        P("grp", "cp"),
        P("cp", None),
        P(None, "cp"),
        P("grp", None),
        P("grp", None),
        P("grp"),
        P("grp"),
    )
    out_specs = (P("grp", None), P("grp", "cp"), P("cp", None))
    return jax.shard_map(
        per_device, mesh=mesh, in_specs=in_specs, out_specs=out_specs, check_vma=False
    )
```

```python
import math

import jax
import jax.numpy as jnp
from jax import lax
from jax.experimental import pallas as pl
from jax.experimental.pallas import tpu as pltpu
from jax.sharding import PartitionSpec as P

HD = 128
ON_MESH = pl.DeviceIdType.MESH

SQRT_HALF = 0.7071067811865476
INV_ROOT_TAU = 0.3989422804014327
NEG_LARGE = -1e30


def remote(source, target, send_sem, recv_sem, where):
    return pltpu.make_async_remote_copy(
        src_ref=source,
        dst_ref=target,
        send_sem=send_sem,
        recv_sem=recv_sem,
        device_id=where,
        device_id_type=ON_MESH,
    )


def greet(peers):
    barrier = pltpu.get_barrier_semaphore()
    for where in peers:
        pl.semaphore_signal(barrier, inc=1, device_id=where, device_id_type=ON_MESH)
    pl.semaphore_wait(barrier, len(peers))


def step_kernel(
    n_cp,
    n_out,
    group_count,
    parts,
    length_hbm,
    action_hbm,
    mask_hbm,
    id_hbm,
    reward_hbm,
    query_ref,
    key_ref,
    value_ref,
    map_ref,
    shard_ref,
    embed_hbm,
    weight_hbm,
    logprob_hbm,
    out_hbm,
    grad_head_hbm,
    length_ref,
    action_ref,
    mask_ref,
    id_ref,
    reward_ref,
    logprob_ref,
    out_ref,
    grad_head_ref,
    heads_all,
    blocks,
    map_held,
    columns_ref,
    frames_ref,
    slope_ref,
    moments,
    pooled_ref,
    embed_ref,
    weight_ref,
    head_rows,
    head_ref,
    logits_send,
    logits_all,
    stats_send,
    stats_all,
    head_all,
    grad_send,
    grad_all,
    pulls,
    pair_send,
    pair_recv,
    line_send,
    line_recv,
    local_sems,
    swap_send,
    swap_recv,
    block_send,
    block_recv,
    shard_send,
    shard_recv,
    pass_send,
    pass_recv,
    logits_sems,
    stats_sems,
    head_sems,
    grad_sems,
    pair_sems,
    line_sends,
    line_recvs,
    scalar_sems,
    out_sems,
):
    episodes, tokens, _ = query_ref.shape
    action_count = action_ref.shape[1]
    width = blocks.shape[2]
    seq = tokens * n_cp
    features, units = columns_ref.shape
    chunk = shard_ref.shape[0]
    rows, bins = logits_send.shape
    span = pair_send.shape[3]
    n_grp = 2 * n_out
    last = n_out - 1
    me, group = lax.axis_index("cp"), lax.axis_index("grp")
    place, core = group // 2, lax.rem(group, 2)
    sibling = 2 * place + 1 - core
    above, below = (me, lax.rem(group + 2, n_grp)), (me, lax.rem(group + n_grp - 2, n_grp))
    square = n_cp == 4
    if square:
        row_peer = me + 1 - 2 * lax.rem(me, 2)
        col_peer = lax.rem(me + 2, 4)
        far_peer = lax.rem(row_peer + 2, 4)
        peers = [far_peer, row_peer, col_peer]
    else:
        peers = [lax.rem(me + step, n_cp) for step in range(1, n_cp)]
    lines = [2 * lax.rem(place + step, n_out) + core for step in range(1, n_out)]
    peers_g = [lax.rem(group + step, n_grp) for step in range(1, n_grp)]

    def shard_rows(owner):
        return columns_ref.at[pl.ds(pl.multiple_of(owner * chunk, 8), chunk), :]

    def my_copy(tensor, source, episode):
        return pltpu.make_async_copy(
            source.at[episode, :, pl.ds(pl.multiple_of(me * width, 128), width)],
            heads_all.at[tensor, episode, pl.ds(pl.multiple_of(me * tokens, 8), tokens), :],
            local_sems.at[4 + tensor * episodes + episode],
        )

    def swap_copy(tensor, source, episode, step, owner, peer):
        return remote(
            source.at[episode, :, pl.ds(pl.multiple_of(peer * width, 128), width)],
            heads_all.at[tensor, episode, pl.ds(pl.multiple_of(owner * tokens, 8), tokens), :],
            swap_send.at[tensor, episode, step],
            swap_recv.at[tensor, episode, owner],
            (peer, group),
        )

    def shard_copy(step, owner, peer):
        return remote(shard_ref, shard_rows(owner), shard_send.at[step], shard_recv.at[owner], (me, peer))

    def pass_copy(step, owner, source):
        return remote(source, shard_rows(owner), pass_send.at[step], pass_recv.at[owner], (me, sibling))

    def to_all(send, everyone, sems, step, owner, where):
        return remote(send, everyone.at[owner], sems.at[0, step], sems.at[1, owner], where)

    sources = (query_ref, key_ref, value_ref)
    map_copy = pltpu.make_async_copy(map_ref, map_held, local_sems.at[0])
    keep_copy = pltpu.make_async_copy(shard_ref, shard_rows(group), local_sems.at[1])
    embed_copy = pltpu.make_async_copy(embed_hbm, embed_ref, local_sems.at[2])
    weight_copy = pltpu.make_async_copy(weight_hbm, weight_ref, local_sems.at[3])

    greet([(peer, group) for peer in peers] + [(me, peer) for peer in peers_g])
    for episode in range(episodes):
        for tensor, source in enumerate(sources):
            for step, peer in enumerate(peers):
                swap_copy(tensor, source, episode, step, me, peer).start()
            my_copy(tensor, source, episode).start()
    for step, peer in reversed(list(enumerate(lines))):
        shard_copy(step, group, peer).start()
    pass_copy(n_out - 1, group, shard_ref).start()
    map_copy.start()
    keep_copy.start()
    embed_copy.start()
    weight_copy.start()

    scalar_copies = [
        pltpu.make_async_copy(source, target, scalar_sems.at[index])
        for index, (source, target) in enumerate(
            [
                (length_hbm, length_ref),
                (action_hbm, action_ref),
                (mask_hbm, mask_ref),
                (id_hbm, id_ref),
                (reward_hbm, reward_ref),
            ]
        )
    ]
    for copy in scalar_copies:
        copy.start()
    for copy in scalar_copies:
        copy.wait()

    lane = lax.broadcasted_iota(jnp.int32, (8, 128), 1)
    stats = jnp.zeros((8, 128), jnp.float32)
    for episode in range(episodes):
        reward, member = reward_ref[episode], id_ref[episode]
        stats = stats + jnp.where(lane == member, reward, 0.0)
        stats = stats + jnp.where(lane == group_count + member, reward * reward, 0.0)
        stats = stats + jnp.where(lane == 2 * group_count + member, 1.0, 0.0)
        for action in range(action_count):
            valid = mask_ref[episode, action].astype(jnp.float32)
            stats = stats + jnp.where(lane == 3 * group_count, valid, 0.0)
    stats_send[...] = stats
    stats_all[group] = stats
    for step, peer in enumerate(peers_g):
        to_all(stats_send, stats_all, stats_sems, step, group, (me, peer)).start()

    pooled_ref[...] = jnp.zeros_like(pooled_ref)
    head_rows[...] = jnp.zeros_like(head_rows)

    tall_query = min(seq, 256)

    def attend(episode):
        live = lax.broadcasted_iota(jnp.int32, (tall_query, seq), 1) < length_ref[episode]

        def one_head(head, carry):
            at = pl.ds(pl.multiple_of(head * HD, HD), HD)
            key_head = heads_all[1, episode, :, at]
            value_head = heads_all[2, episode, :, at]
            for first in range(0, seq, tall_query):
                query_head = heads_all[0, episode, first : first + tall_query, at]
                scores = lax.dot_general(
                    query_head, key_head, (((1,), (1,)), ((), ())), preferred_element_type=jnp.float32
                )
                scores = jnp.where(live, scores * (1.0 / math.sqrt(HD)), NEG_LARGE)
                probs = jnp.exp(scores - jnp.max(scores, axis=1, keepdims=True))
                row_total = jnp.sum(probs, axis=1, keepdims=True)
                weighted = jnp.dot(probs.astype(jnp.bfloat16), value_head, preferred_element_type=jnp.float32)
                blocks[me, episode * seq + first : episode * seq + first + tall_query, at] = (
                    weighted / row_total
                ).astype(jnp.bfloat16)
            return carry

        lax.fori_loop(0, width // HD, one_head, 0)

    tile = min(units, 512)
    per_band = units // tile
    bands = -(-features // (tile * per_band))
    staged = square and episodes == 2 and bands * seq <= features and seq % 128 == 0

    def add_frames(episode, first, tall, owners, opens, closes):
        for index, left in enumerate(range(0, features, tile)):
            lanes = min(tile, features - left)
            part = None
            for owner in owners:
                term = jnp.dot(
                    blocks[owner, episode * seq + first : episode * seq + first + tall, :],
                    map_held[pl.ds(pl.multiple_of(owner * width, 128), width), left : left + lanes],
                    preferred_element_type=jnp.float32,
                )
                part = term if part is None else part + term
            down, across = index // per_band * seq + first, index % per_band * tile
            held = (episode, slice(down, down + tall), slice(across, across + lanes))
            if not opens:
                part = part + moments[held]
            if closes:
                frames_ref[episode, first : first + tall, left : left + lanes] = part.astype(jnp.bfloat16)
            else:
                moments[held] = part

    def activate(episode, first, tall):
        length = jnp.full((tall, 1), length_ref[episode], jnp.int32)
        kept = lax.broadcasted_iota(jnp.int32, (tall, 1), 0) + first < length
        scale = jnp.where(kept, 1.0 / length.astype(jnp.float32), 0.0)
        for left in range(0, units, tile):
            at = slice(left, left + tile)
            pre_act = jnp.dot(
                frames_ref[episode, first : first + tall, :],
                columns_ref[:, at],
                preferred_element_type=jnp.float32,
            )
            below_it = 0.5 * (1.0 + lax.erf(pre_act * SQRT_HALF))
            pooled_ref[episode : episode + 1, at] += jnp.sum(
                scale * (pre_act * below_it), axis=0, keepdims=True
            )
            slope = below_it + pre_act * jnp.exp(-0.5 * pre_act * pre_act) * INV_ROOT_TAU
            slope_ref[episode, first : first + tall, at] = (scale * slope).astype(jnp.bfloat16)

    def find_moments(episode):
        for left in range(0, features, 256):
            at = slice(left, min(left + 256, features))
            moments[episode, at, :] = lax.dot_general(
                frames_ref[episode, :, at],
                slope_ref[episode],
                (((0,), (0,)), ((), ())),
                preferred_element_type=jnp.float32,
            )

    def wait_heads(episode):
        for tensor, source in enumerate(sources):
            my_copy(tensor, source, episode).wait()
            for peer in peers:
                swap_copy(tensor, source, episode, 0, peer, peer).wait_recv()

    def forward_shards():
        for step, peer in enumerate(lines):
            shard_copy(step, peer, peer).wait_recv()
            pass_copy(step, peer, columns_ref.at[pl.ds(pl.multiple_of(peer * chunk, 8), chunk), :]).start()

    def wait_columns():
        for step, peer in enumerate(lines):
            pass_copy(step, peer + 1 - 2 * core, shard_rows(peer)).wait_recv()
        pass_copy(n_out - 1, sibling, shard_ref).wait_recv()
        keep_copy.wait()

    def block_copy(strip, step, owner, peer, at, part):
        held = blocks.at[owner, pl.ds(*at), :]
        return remote(held, held, block_send.at[strip, step], block_recv.at[strip, owner, part], (peer, group))

    if staged:
        strips = [(0, first, seq // 2) for first in range(0, seq, seq // 2)]
        strips += [(1, first, seq // 4) for first in range(0, seq, seq // 4)]

        def whole_of(strip):
            episode, first, tall = strips[strip]
            return episode * seq + first, tall

        def half_of(strip, which):
            start, tall = whole_of(strip)
            return start + which * (tall // 2), tall // 2

        def own(strip):
            block_copy(strip, 0, me, row_peer, whole_of(strip), 0).start()
            block_copy(strip, 1, me, col_peer, whole_of(strip), 0).start()

        def forward(strip):
            block_copy(strip, 0, row_peer, row_peer, whole_of(strip), 0).wait_recv()
            block_copy(strip, 2, row_peer, col_peer, half_of(strip, 0), 0).start()
            block_copy(strip, 1, col_peer, col_peer, whole_of(strip), 0).wait_recv()
            block_copy(strip, 3, col_peer, row_peer, half_of(strip, 1), 1).start()

        def add_near(strip):
            add_frames(*strips[strip], [me, row_peer, col_peer], True, False)

        def add_far(strip):
            block_copy(strip, 2, far_peer, col_peer, half_of(strip, 0), 0).wait_recv()
            block_copy(strip, 3, far_peer, row_peer, half_of(strip, 1), 1).wait_recv()
            add_frames(*strips[strip], [far_peer], False, True)

        wait_heads(0)
        attend(0)
        own(0)
        own(1)
        wait_heads(1)
        attend(1)
        map_copy.wait()
        forward(0)
        add_near(0)
        forward(1)
        own(2)
        own(3)
        add_near(1)
        forward_shards()
        add_far(0)
        add_far(1)
        wait_columns()
        activate(*strips[0])
        forward(2)
        own(4)
        add_near(2)
        activate(*strips[1])
        forward(3)
        own(5)
        add_near(3)
        add_far(2)
        activate(*strips[2])
        find_moments(0)
        forward(4)
        add_near(4)
        add_far(3)
        activate(*strips[3])
        forward(5)
        add_near(5)
        add_far(4)
        activate(*strips[4])
        add_far(5)
        activate(*strips[5])
    else:
        tall = min(seq, 128)
        for episode in range(episodes):
            wait_heads(episode)
            attend(episode)
            for step, peer in enumerate(peers):
                block_copy(episode, step, me, peer, (episode * seq, seq), 0).start()
        map_copy.wait()
        forward_shards()
        wait_columns()
        for episode in range(episodes):
            for step, peer in enumerate(peers):
                block_copy(episode, step, peer, peer, (episode * seq, seq), 0).wait_recv()
            for first in range(0, seq, tall):
                add_frames(episode, first, tall, [me] + peers, True, True)
                activate(episode, first, tall)
            if episode < episodes - 1:
                find_moments(episode)

    embed_copy.wait()
    weight_copy.wait()
    for episode in range(episodes):
        head_rows[episode * action_count : (episode + 1) * action_count, :] = (
            pooled_ref[episode : episode + 1, :] + embed_ref[...]
        )
    head_ref[...] = head_rows[...].astype(jnp.bfloat16)
    partial = jnp.dot(head_ref[...], weight_ref[...], preferred_element_type=jnp.float32)
    logits_send[...] = partial
    logits_all[me] = partial
    for step, peer in enumerate(peers):
        to_all(logits_send, logits_all, logits_sems, step, me, (peer, group)).start()
    head_all[group] = head_ref[...]
    for step, peer in enumerate(peers_g):
        to_all(head_ref, head_all, head_sems, step, group, (me, peer)).start()

    find_moments(episodes - 1)

    for peer in peers_g:
        to_all(stats_send, stats_all, stats_sems, 0, peer, (me, peer)).wait_recv()
    stats = jnp.sum(stats_all[...], axis=0)[0:1]
    lane = lane[0:1]

    def entry(index):
        return jnp.sum(jnp.where(lane == index, stats, 0.0), axis=1, keepdims=True)

    mask_total = jnp.maximum(entry(3 * group_count), 1.0)
    row = lax.broadcasted_iota(jnp.int32, (rows, 1), 0)
    chosen = jnp.zeros((rows, 1), jnp.int32)
    loss_weight = jnp.zeros((rows, 1), jnp.float32)
    for episode in range(episodes):
        member = id_ref[episode]
        size = jnp.maximum(entry(2 * group_count + member), 1.0)
        mean = entry(member) / size
        variance = entry(group_count + member) / size - mean * mean
        advantage = (reward_ref[episode] - mean) / jnp.sqrt(jnp.maximum(variance, 1.0))
        for action in range(action_count):
            here = row == episode * action_count + action
            chosen = jnp.where(here, action_ref[episode, action], chosen)
            valid = mask_ref[episode, action].astype(jnp.float32)
            loss_weight = jnp.where(here, -valid * advantage / mask_total, loss_weight)
    picked = (lax.broadcasted_iota(jnp.int32, (rows, bins), 1) == chosen).astype(jnp.float32)

    for peer in peers:
        to_all(logits_send, logits_all, logits_sems, 0, peer, (peer, group)).wait_recv()
    logits = logits_all[0]
    for slot in range(1, n_cp):
        logits = logits + logits_all[slot]
    shifted = logits - jnp.max(logits, axis=1, keepdims=True)
    log_all = shifted - jnp.log(jnp.sum(jnp.exp(shifted), axis=1, keepdims=True))
    logprob = jnp.sum(picked * log_all, axis=1, keepdims=True)
    logit_grad = (loss_weight * (picked - jnp.exp(log_all))).astype(jnp.bfloat16)
    grad_send[...] = logit_grad
    mates = lines + [sibling]
    for step, peer in enumerate(mates):
        to_all(grad_send, grad_all, grad_sems, step, group, (me, peer)).start()
    pull_back = lax.dot_general(
        logit_grad, weight_ref[...], (((1,), (1,)), ((), ())), preferred_element_type=jnp.float32
    )
    for episode in range(episodes):
        mine = jnp.logical_and(row >= episode * action_count, row < (episode + 1) * action_count)
        pulls[episode : episode + 1, :] = jnp.sum(jnp.where(mine, pull_back, 0.0), axis=0, keepdims=True)

    block = 16 if chunk % 16 == 0 else 8

    def fill(target, slot, part, terms):
        at = pl.ds(pl.multiple_of(part * span, 128), span)
        scales = [pulls[episode : episode + 1, at] for episode in range(episodes)]

        def some(index, carry):
            here = pl.ds(pl.multiple_of(index * block, block), block)
            down = pl.ds(pl.multiple_of(slot * chunk + index * block, 8), block)
            total = moments[0, down, at] * scales[0]
            for episode in range(1, episodes):
                total = total + moments[episode, down, at] * scales[episode]
            for term in terms:
                total = total + term[here, :].astype(jnp.float32)
            target[here, :] = total.astype(jnp.bfloat16)
            return carry

        lax.fori_loop(0, chunk // block, some, 0, unroll=True)

    def pair_copy(target, part):
        return remote(
            pair_send.at[target, part],
            pair_recv.at[target, part],
            pair_sems.at[0, target, part],
            pair_sems.at[1, target, part],
            (me, sibling),
        )

    def line_copy(slot, part, where):
        return remote(
            line_send.at[slot, part],
            line_recv.at[slot, part],
            line_sends.at[slot, part],
            line_recvs.at[slot, part],
            where,
        )

    def up_copy(target, part):
        return line_copy(target + 1, part, above)

    def down_copy(target, part):
        return line_copy(target, part, below)

    def give(target, part):
        fill(pair_send.at[target, part], 2 * target + 1 - core, part, [])
        pair_copy(target, part).start()

    def pass_on(target, part, slot, ends, copy):
        pair_copy(target, part).wait_recv()
        own_part = [pair_recv.at[target, part]]
        goal = line_send.at[slot, part]

        @pl.when(ends)
        def _():
            fill(goal, 2 * target + core, part, own_part)

        @pl.when(jnp.logical_not(ends))
        def _():
            copy(target, part).wait_recv()
            fill(goal, 2 * target + core, part, own_part + [line_recv.at[slot, part]])

        copy(target, part).start()

    steps = last * parts

    def give_at(index):
        time, part = lax.div(index, parts), lax.rem(index, parts)
        early = index < steps

        @pl.when(jnp.logical_and(early, time >= place))
        def _():
            give(last + place - time, part)

        @pl.when(jnp.logical_and(early, time >= last - place))
        def _():
            give(time - last + place, part)

        @pl.when(jnp.logical_not(early))
        def _():
            give(place, index - steps)

    def pass_at(index):
        time, part = lax.div(index, parts), lax.rem(index, parts)

        @pl.when(time >= place)
        def _():
            target = last + place - time
            pass_on(target, part, target + 1, place == 0, up_copy)

        @pl.when(time >= last - place)
        def _():
            target = time - last + place
            pass_on(target, part, target, place == last, down_copy)

    def open_up(index, carry):
        give_at(index)
        return carry

    def go_on(index, carry):
        give_at(index + parts)
        pass_at(index)
        return carry

    lax.fori_loop(0, parts, open_up, 0)
    lax.fori_loop(0, steps, go_on, 0)

    grad_all[group] = logit_grad
    for step, peer in enumerate(lines):
        to_all(grad_send, grad_all, grad_sems, 0, peer, (me, peer)).wait_recv()
        to_all(grad_all.at[peer], grad_all, grad_sems, n_out + step, peer, (me, sibling)).start()

    cell = lax.broadcasted_iota(jnp.int32, (episodes, action_count), 0) * action_count
    cell = cell + lax.broadcasted_iota(jnp.int32, (episodes, action_count), 1)
    laid = jnp.zeros((episodes, action_count), jnp.float32)
    for index in range(episodes * action_count):
        laid = jnp.where(cell == index, logprob[index : index + 1, :], laid)
    logprob_ref[...] = laid
    logprob_out = pltpu.make_async_copy(logprob_ref, logprob_hbm, out_sems.at[0])
    logprob_out.start()
    for peer in peers_g:
        to_all(head_ref, head_all, head_sems, 0, peer, (me, peer)).wait_recv()
    to_all(grad_send, grad_all, grad_sems, 0, sibling, (me, sibling)).wait_recv()
    for step, peer in enumerate(lines):
        other = peer + 1 - 2 * core
        to_all(grad_send, grad_all, grad_sems, 0, other, (me, sibling)).wait_recv()
    grad_head_ref[...] = lax.dot_general(
        head_all[...].reshape(n_grp * rows, units),
        grad_all[...].reshape(n_grp * rows, bins),
        (((0,), (0,)), ((), ())),
        preferred_element_type=jnp.float32,
    ).astype(jnp.bfloat16)
    grad_head_out = pltpu.make_async_copy(grad_head_ref, grad_head_hbm, out_sems.at[1])
    grad_head_out.start()

    def out_copy(part):
        at = pl.ds(part * span, span)
        return pltpu.make_async_copy(out_ref.at[:, at], out_hbm.at[:, at], out_sems.at[2 + part])

    for part in range(parts):
        goal = out_ref.at[:, pl.ds(part * span, span)]
        pair_copy(place, part).wait_recv()
        own_part = [pair_recv.at[place, part]]
        rose, fell = line_recv.at[place + 1, part], line_recv.at[place, part]

        @pl.when(place == 0)
        def _():
            down_copy(place, part).wait_recv()
            fill(goal, group, part, own_part + [fell])

        @pl.when(place == last)
        def _():
            up_copy(place, part).wait_recv()
            fill(goal, group, part, own_part + [rose])

        @pl.when(jnp.logical_and(place > 0, place < last))
        def _():
            up_copy(place, part).wait_recv()
            down_copy(place, part).wait_recv()
            fill(goal, group, part, own_part + [rose, fell])

        out_copy(part).start()

    for target in range(n_out):
        for part in range(parts):
            pair_copy(target, part).wait_send()

            @pl.when(target > place)
            def _():
                up_copy(target, part).wait_send()

            @pl.when(target < place)
            def _():
                down_copy(target, part).wait_send()

    for step, peer in enumerate(peers):
        to_all(logits_send, logits_all, logits_sems, step, me, (peer, group)).wait_send()
    for step, peer in enumerate(peers_g):
        to_all(stats_send, stats_all, stats_sems, step, group, (me, peer)).wait_send()
        to_all(head_ref, head_all, head_sems, step, group, (me, peer)).wait_send()
    for step, peer in enumerate(mates):
        to_all(grad_send, grad_all, grad_sems, step, group, (me, peer)).wait_send()
    for step, peer in enumerate(lines):
        to_all(grad_all.at[peer], grad_all, grad_sems, n_out + step, peer, (me, sibling)).wait_send()
    for episode in range(episodes):
        for tensor, source in enumerate(sources):
            for step, peer in enumerate(peers):
                swap_copy(tensor, source, episode, step, me, peer).wait_send()
    if staged:
        for strip in range(len(strips)):
            block_copy(strip, 0, me, row_peer, whole_of(strip), 0).wait_send()
            block_copy(strip, 1, me, col_peer, whole_of(strip), 0).wait_send()
            block_copy(strip, 2, row_peer, col_peer, half_of(strip, 0), 0).wait_send()
            block_copy(strip, 3, col_peer, row_peer, half_of(strip, 1), 1).wait_send()
    else:
        for episode in range(episodes):
            for step, peer in enumerate(peers):
                block_copy(episode, step, me, peer, (episode * seq, seq), 0).wait_send()
    for step, peer in enumerate(lines):
        shard_copy(step, group, peer).wait_send()
        pass_copy(step, peer, shard_rows(peer)).wait_send()
    pass_copy(n_out - 1, group, shard_ref).wait_send()
    logprob_out.wait()
    grad_head_out.wait()
    for part in range(parts):
        out_copy(part).wait()


def train_step(
    queries,
    keys,
    values,
    lengths,
    frame_map,
    proj_weight,
    head_weight,
    act_embed,
    actions,
    action_mask,
    group_ids,
    rewards,
):
    n_cp, n_grp = lax.axis_size("cp"), lax.axis_size("grp")
    n_out = n_grp // 2
    episodes, tokens, att_width = queries.shape
    group_count = max(1, episodes * n_grp // 8)
    seq, width = tokens * n_cp, att_width // n_cp
    chunk, units = proj_weight.shape
    features = frame_map.shape[1]
    rows, bins = -(-actions.size // 16) * 16, head_weight.shape[1]
    parts = 2
    strips = episodes + 4
    anywhere = pl.BlockSpec(memory_space=pl.ANY)
    dma = pltpu.SemaphoreType.DMA
    bf16, f32 = jnp.bfloat16, jnp.float32
    return pl.pallas_call(
        lambda *refs: step_kernel(n_cp, n_out, group_count, parts, *refs),
        out_shape=(
            jax.ShapeDtypeStruct(actions.shape, f32),
            jax.ShapeDtypeStruct((chunk, units), bf16),
            jax.ShapeDtypeStruct((units, bins), bf16),
        ),
        in_specs=[anywhere] * 12,
        out_specs=(anywhere,) * 3,
        scratch_shapes=[
            pltpu.SMEM(lengths.shape, lengths.dtype),
            pltpu.SMEM(actions.shape, actions.dtype),
            pltpu.SMEM(action_mask.shape, action_mask.dtype),
            pltpu.SMEM(group_ids.shape, group_ids.dtype),
            pltpu.SMEM(rewards.shape, f32),
            pltpu.VMEM(actions.shape, f32),
            pltpu.VMEM((chunk, units), bf16),
            pltpu.VMEM((units, bins), bf16),
            pltpu.VMEM((3, episodes, seq, width), bf16),
            pltpu.VMEM((n_cp, episodes * seq, width), bf16),
            pltpu.VMEM(frame_map.shape, bf16),
            pltpu.VMEM((n_grp * chunk, units), bf16),
            pltpu.VMEM((episodes, seq, features), bf16),
            pltpu.VMEM((episodes, seq, units), bf16),
            pltpu.VMEM((episodes, features, units), f32),
            pltpu.VMEM((-(-episodes // 8) * 8, units), f32),
            pltpu.VMEM(act_embed.shape, f32),
            pltpu.VMEM(head_weight.shape, bf16),
            pltpu.VMEM((rows, units), f32),
            pltpu.VMEM((rows, units), bf16),
            pltpu.VMEM((rows, bins), f32),
            pltpu.VMEM((n_cp, rows, bins), f32),
            pltpu.VMEM((8, 128), f32),
            pltpu.VMEM((n_grp, 8, 128), f32),
            pltpu.VMEM((n_grp, rows, units), bf16),
            pltpu.VMEM((rows, bins), bf16),
            pltpu.VMEM((n_grp, rows, bins), bf16),
            pltpu.VMEM((-(-episodes // 8) * 8, units), f32),
            pltpu.VMEM((n_out, parts, chunk, units // parts), bf16),
            pltpu.VMEM((n_out, parts, chunk, units // parts), bf16),
            pltpu.VMEM((n_out + 1, parts, chunk, units // parts), bf16),
            pltpu.VMEM((n_out + 1, parts, chunk, units // parts), bf16),
            dma((4 + 3 * episodes,)),
            dma((3, episodes, n_cp)),
            dma((3, episodes, n_cp)),
            dma((strips, max(n_cp, 4))),
            dma((strips, n_cp, 2)),
            dma((n_out,)),
            dma((n_grp,)),
            dma((n_out,)),
            dma((n_grp,)),
            dma((2, n_cp)),
            dma((2, n_grp)),
            dma((2, n_grp)),
            dma((2, n_grp)),
            dma((2, n_out, parts)),
            dma((n_out + 1, parts)),
            dma((n_out + 1, parts)),
            dma((5,)),
            dma((2 + parts,)),
        ],
        compiler_params=pltpu.CompilerParams(
            collective_id=1, has_side_effects=True, vmem_limit_bytes=62 * 1024 * 1024
        ),
        name="train_step",
    )(
        lengths,
        actions,
        action_mask,
        group_ids,
        rewards,
        queries,
        keys,
        values,
        frame_map,
        proj_weight,
        act_embed,
        head_weight,
    )


def write_kernel(first, second, third, first_out, second_out, third_out):
    first_out[...] = first[...]
    second_out[...] = second[...]
    third_out[...] = third[...]


def write_out(*results):
    in_vmem = pl.BlockSpec(memory_space=pltpu.VMEM)
    return pl.pallas_call(
        write_kernel,
        out_shape=tuple(jax.ShapeDtypeStruct(result.shape, result.dtype) for result in results),
        in_specs=[in_vmem] * 3,
        out_specs=(in_vmem,) * 3,
        name="write_out",
    )(*results)


def per_device(*arrays):
    return write_out(*train_step(*arrays))


def solution(mesh):
    in_specs = (
        P("grp", "cp", None),
        P("grp", "cp", None),
        P("grp", "cp", None),
        P("grp"),
        P(),
        P("grp", "cp"),
        P("cp", None),
        P(None, "cp"),
        P("grp", None),
        P("grp", None),
        P("grp"),
        P("grp"),
    )
    out_specs = (P("grp", None), P("grp", "cp"), P("cp", None))
    return jax.shard_map(
        per_device, mesh=mesh, in_specs=in_specs, out_specs=out_specs, check_vma=False
    )
```
